32 devices in a mesh: group: 2 (over y), tok: 4 (over z), qp: 2 (over x), rep: 2 (over core).
Axes of the slice: x: 2, y: 2, z: 4, core: 2. Of those that a mesh axis runs over, the one named last changes fastest.
Arguments:
- tokens: bfloat16 [6144, 1024], P(('group', 'tok', 'qp', 'rep')), parts along dimension 0, may hold values from -6 to 6
- listed: int32 [32, 8, 10], P(('group', 'tok', 'qp', 'rep')), parts along dimension 0, may hold values from -1 to 191, as said below
- w_qkv: bfloat16 [8, 1024, 384], P(('tok', 'rep')), may hold values from -0.1875 to 0.1875
- w_out: bfloat16 [8, 128, 1024], P(('tok', 'rep')), may hold values from -0.5 to 0.5
- w_select: bfloat16 [8, 1024], P(('tok', 'rep')), may hold values from -0.1875 to 0.1875
- norm_gain: bfloat16 [1024], replicated, may hold values from 0.25 to 1.75
- expert_id: int32 [6144, 1], P(('group', 'tok', 'qp', 'rep')), parts along dimension 0, may hold values from 0 to 7; in each aligned block of 192 rows (0 to 191, 192 to 383, ...) at most 48 rows name the same one
- router: bfloat16 [8, 1024], P(('tok', 'qp')), may hold values from -0.1875 to 0.1875
- w_gate: bfloat16 [8, 1024, 1024], P(('tok', 'qp'), None, 'rep'), may hold values from -0.1875 to 0.1875
- w_up: bfloat16 [8, 1024, 1024], P(('tok', 'qp'), None, 'rep'), may hold values from -0.1875 to 0.1875
- w_down: bfloat16 [8, 1024, 1024], P(('tok', 'qp'), 'rep'), may hold values from -0.1875 to 0.1875
Outputs:
- mixed: bfloat16 [6144, 1024], P(('group', 'tok', 'qp', 'rep')), parts along dimension 0
The draws below stay inside these ranges and needn't reach their ends.
There are 2 independent parts, one for each index of `group`. The reference program is written for one: setup_inputs(seed, part) draws one part's arguments, and reference() takes and returns one part's arrays. A program takes and returns all parts, laid end to end along the dimension named above; an argument that names none is the same for every part. Nothing has to cross between parts.
Inputs may be any that keep to these rules, and one draw needn't show every extreme that they name: listed[b, h] gives, in ascending order, the positions within block b of the tokens head h lists there, then -1 entries; every head lists 128 tokens in all. In every draw some head lists exactly 10 tokens in every block of one set of blocks that share their qp index. `expert_id`: among the 192 tokens of one block no expert is named more than 48 times; in some block some expert is named exactly 48 times.
All inputs are finite; a program needn't handle non-finite values.
Results may differ from the reference program's by a relative error of at most 0.004.
Values may be sent and summed in bfloat16 or wider, within the bound.
A program may use at most 64 MiB of HBM per device.

```python
import math
import jax
import jax.numpy as jnp
import numpy as np
from jax import lax

D = 1024
HD = 128
FF = 1024
KBLK = 8
CAP_H = 10
TOK_DEV = 192
H = 8
EXPERTS = 8
NBLK = 16
S = 3072
CAP_E = 48
N_TOK = 4
N_QP = 2
N_REP = 2


def shuffle_rows(row_key):
    return jax.random.permutation(row_key, TOK_DEV)


def draw_listed(key, part):
    spread_width = CAP_H - KBLK
    half_panels = N_QP // 2
    shift_key, head_key, panel_key, order_key = jax.random.split(key, 4)
    shifts = jax.random.randint(shift_key, (H, N_TOK, half_panels, N_REP), -spread_width, spread_width + 1)
    full_head = jax.random.randint(head_key, (), 0, H)
    full_panel = jax.random.randint(panel_key, (), 0, half_panels)
    forced = (jnp.arange(H)[:, None, None, None] == full_head) & (jnp.arange(half_panels)[None, None, :, None] == full_panel)
    shifts = jnp.where(forced, spread_width, shifts)
    counts = jnp.concatenate([KBLK + shifts, KBLK - shifts], axis=2).reshape(H, NBLK)
    order_keys = jax.random.split(order_key, NBLK * H)
    orders = jax.vmap(shuffle_rows)(order_keys).reshape(NBLK, H, TOK_DEV)
    chosen = jnp.where(jnp.arange(TOK_DEV)[None, None, :] < jnp.transpose(counts)[:, :, None], orders, 2 * TOK_DEV)
    ordered = jnp.sort(chosen, axis=2)[:, :, :CAP_H]
    return jnp.where(ordered >= TOK_DEV, -1, ordered).astype(jnp.int32)


def shard_levels(key, shape, cuts, smallest, top_value):
    gain, own = 1.0, jax.random.fold_in(key, 6)
    for axis_at, shards_of in cuts:
        draws = jnp.exp(jax.random.uniform(jax.random.fold_in(own, axis_at), (shards_of,), jnp.float32, smallest / len(cuts), top_value / len(cuts)))
        gain = gain * jnp.repeat(draws, shape[axis_at] // shards_of).reshape([-1 if axis == axis_at else 1 for axis in range(len(shape))])
    return gain


def deal_out(rng, own, number, rows, count, top, bound, lean):
    sequence = jax.random.permutation(rng, count)
    packed, common = load_shares(count, rows * top, bound, lean, True), load_shares(count, rows * top, bound, lean, False)
    places = jnp.arange(count)

    def named(tallies, turn):
        used = int((tallies > 0).sum())
        fixed = max(1, used // 4)
        moved = fixed + (places - fixed + turn * (used - fixed)) % max(1, count - fixed)
        return jnp.zeros((count,), jnp.int32).at[sequence[jnp.where(places < fixed, places, moved)]].set(jnp.asarray(tallies, jnp.int32))

    tallies = jnp.where(number % 4 == 0, named(packed, number // 4), named(common, number - number // 4 - 1))
    mixed = jax.random.permutation(jax.random.fold_in(own, 3), count)
    giver, sink = mixed[0:count // 2 * 2:2], mixed[1:count // 2 * 2:2]
    slack = jnp.minimum(tallies[giver] - 1, bound - tallies[sink]) // 2
    slack = jnp.where((giver == sequence[0]) | (sink == sequence[0]) | (tallies[sink] == 0), 0, jnp.maximum(slack, 0))
    moved = jax.random.randint(jax.random.fold_in(own, 4), (count // 2,), 0, 1 << 20) % (slack + 1)
    tallies = tallies.at[giver].add(-moved).at[sink].add(moved)
    members = jnp.searchsorted(jnp.cumsum(tallies), jnp.arange(rows * top), side="right").astype(jnp.int32)
    grid = members.reshape(top, rows).T
    grid = grid[jax.random.permutation(jax.random.fold_in(own, 1), rows)]
    turn = jax.random.randint(jax.random.fold_in(own, 2), (rows, 1), 0, top)
    return jnp.take_along_axis(grid, (jnp.arange(top)[None, :] + turn) % top, axis=1)


def load_shares(amount, total, bound, lean, full):
    portions = [(1 << 20) // math.isqrt(standing ** lean) + 1 for standing in range(1, amount + 1)]
    largest = bound if full else min(bound, max(-(-total // amount), total * portions[0] // sum(portions)))
    least = 1 if total - largest >= amount - 1 else 0
    given, rest = [largest] + [least] * (amount - 1), total - largest - least * (amount - 1)
    while rest > 0:
        free = [i for i in range(1, amount) if given[i] < largest] or [i for i in range(1, amount) if given[i] < bound]
        mass, remaining = sum([portions[i] for i in free]), rest
        for i in free:
            more = min(bound - given[i], max(1, remaining * portions[i] // mass), rest)
            given[i] = given[i] + more
            rest = rest - more
    return np.array(given)


def gaussian(key, dims, deviation, reach, pieces=(), held_as=jnp.bfloat16):
    gain = shard_levels(key, dims, pieces, -0.22, 0.18) if pieces else 1.0
    drawn = jax.random.normal(key, dims, jnp.float32) * deviation * gain
    return jnp.minimum(jnp.maximum(drawn, -reach), reach).astype(held_as)


def setup_inputs(seed: int = 0, part: int = 0) -> dict:
    arg_keys = jax.random.split(jax.random.key(seed), 12)
    own_keys = jax.random.split(jax.random.fold_in(arg_keys[11], part), 12)
    tokens = gaussian(own_keys[0], (S, D), 1.0, 6.0, ((0, 16),))
    listed = draw_listed(jax.random.fold_in(jax.random.fold_in(arg_keys[11], part), 71), part)
    w_qkv = gaussian(arg_keys[2], (H, D, 3 * HD), D ** -0.5, 0.1875, ((0, 8),))
    w_out = gaussian(arg_keys[3], (H, HD, D), HD ** -0.5, 0.5, ((0, 8),))
    w_select = gaussian(arg_keys[4], (H, D), D ** -0.5, 0.1875, ((0, 8),))
    norm_gain = jnp.clip(1.0 + 0.15 * jax.random.normal(arg_keys[5], (D,), jnp.float32), 0.25, 1.75).astype(jnp.bfloat16)
    expert_id_keys = jax.random.split(jax.random.fold_in(own_keys[6], 1), S // TOK_DEV)
    expert_id_turns = jax.random.permutation(jax.random.fold_in(own_keys[6], 3), S // TOK_DEV)
    expert_id = jax.vmap(lambda own, number: deal_out(jax.random.fold_in(own_keys[6], 2), own, number, TOK_DEV, EXPERTS, 1, CAP_E, 1))(expert_id_keys, expert_id_turns).reshape((S, 1))
    router = gaussian(arg_keys[7], (EXPERTS, D), D ** -0.5, 0.1875, ((0, 8),))
    w_gate = gaussian(arg_keys[8], (EXPERTS, D, FF), D ** -0.5, 0.1875, ((0, 8), (2, 2)))
    w_up = gaussian(arg_keys[9], (EXPERTS, D, FF), D ** -0.5, 0.1875, ((0, 8), (2, 2)))
    w_down = gaussian(arg_keys[10], (EXPERTS, FF, D), FF ** -0.5, 0.1875, ((0, 8), (1, 2)))
    return dict(tokens=tokens, listed=listed, w_qkv=w_qkv, w_out=w_out, w_select=w_select, norm_gain=norm_gain, expert_id=expert_id, router=router, w_gate=w_gate, w_up=w_up, w_down=w_down)


def unit_rms(values):
    return values * lax.rsqrt(lax.optimization_barrier(jnp.mean(values * values, axis=-1, keepdims=True)) + 1e-06)

def expert_terms(flat_rows, gate_weight, up_weight, down_weight):
    gate_value = jnp.dot(flat_rows, gate_weight, preferred_element_type=jnp.float32)
    up_value = jnp.dot(flat_rows, up_weight, preferred_element_type=jnp.float32)
    hidden = (jax.nn.silu(gate_value) * up_value).astype(jnp.bfloat16)
    return jnp.dot(hidden, down_weight, preferred_element_type=jnp.float32)

def reference(tokens, listed, w_qkv, w_out, w_select, norm_gain, expert_id, router, w_gate, w_up, w_down):
    all_tokens = tokens.shape[0]
    model_width = tokens.shape[1]
    block_count = listed.shape[0]
    block_rows = all_tokens // block_count
    head_width = w_out.shape[1]

    def head_pass(attention, inputs):
        head_list, head_project, head_output, head_select = inputs
        is_listed = (head_list >= 0).reshape(-1)
        token_index = (jnp.arange(block_count, dtype=jnp.int32)[:, None] * block_rows + jnp.maximum(head_list, 0)).reshape(-1).astype(jnp.int32)
        positions = jnp.where(is_listed, token_index, all_tokens).astype(jnp.int32)
        head_rows = jnp.where(is_listed[:, None], tokens[token_index], jnp.zeros((), jnp.bfloat16))
        projected = jnp.dot(head_rows, head_project, preferred_element_type=jnp.float32)
        queries = unit_rms(projected[:, :head_width]).astype(jnp.bfloat16)
        key_rows = unit_rms(projected[:, head_width:2 * head_width]).astype(jnp.bfloat16)
        value_rows = projected[:, 2 * head_width:].astype(jnp.bfloat16)
        head_gate = jax.nn.sigmoid(jnp.dot(head_rows, head_select, preferred_element_type=jnp.float32))
        scores = jnp.dot(queries, key_rows.T, preferred_element_type=jnp.float32) * head_width ** (-0.5)
        weights = jnp.where(positions[None, :] <= positions[:, None], jnp.exp(scores), 0.0)
        numerator = jnp.dot(weights.astype(jnp.bfloat16), value_rows, preferred_element_type=jnp.float32)
        attended = (numerator / lax.optimization_barrier(jnp.sum(weights, axis=1, keepdims=True))).astype(jnp.bfloat16)
        contribution = (jnp.dot(attended, head_output, preferred_element_type=jnp.float32) * head_gate[:, None]).astype(jnp.bfloat16)
        attention = attention.at[positions].add(contribution.astype(jnp.float32), mode='drop')
        return (attention, None)
    attention, unused = lax.scan(head_pass, jnp.zeros((all_tokens, model_width), jnp.float32), (jnp.transpose(listed, (1, 0, 2)), w_qkv, w_out, w_select))
    residual = tokens.astype(jnp.float32) + attention
    normed = (unit_rms(residual) * norm_gain.astype(jnp.float32)).astype(jnp.bfloat16)
    expert_count = router.shape[0]
    expert_of = expert_id[:, 0].reshape(block_count, block_rows)
    onehot = (expert_of[:, :, None] == jnp.arange(expert_count, dtype=jnp.int32)[None, None, :]).astype(jnp.int32)
    running = jnp.cumsum(onehot, axis=1)
    slot_of = (lax.optimization_barrier(jnp.sum(running * onehot, axis=2)) - 1).astype(jnp.int32)
    slot_key = (expert_of * CAP_E + slot_of).astype(jnp.int32)
    block_ids = jnp.broadcast_to(jnp.arange(block_count, dtype=jnp.int32)[:, None], (block_count, block_rows))
    buffers = jnp.zeros((block_count, expert_count * CAP_E, model_width), jnp.bfloat16)
    buffers = buffers.at[block_ids, slot_key].set(normed.reshape(block_count, block_rows, model_width))
    by_expert = jnp.transpose(buffers.reshape(block_count, expert_count, CAP_E, model_width), (1, 0, 2, 3))
    by_expert = by_expert.reshape(expert_count, block_count * CAP_E, model_width)

    def expert_pass(inputs):
        expert_rows, gate_weight, up_weight, down_weight, router_row = inputs
        expert_out = expert_terms(expert_rows, gate_weight, up_weight, down_weight)
        router_gate = jax.nn.sigmoid(jnp.dot(expert_rows, router_row, preferred_element_type=jnp.float32))
        return (expert_out * router_gate[:, None]).astype(jnp.bfloat16)
    outputs = lax.map(expert_pass, (by_expert, w_gate, w_up, w_down, router))
    outputs = outputs.reshape(expert_count, block_count, CAP_E, model_width)
    routed = outputs[expert_of, block_ids, slot_of].reshape(all_tokens, model_width)
    return (residual + routed.astype(jnp.float32)).astype(jnp.bfloat16)
```

```python
import functools
import jax
import jax.numpy as jnp
from jax import lax
from jax.experimental import pallas as pl
from jax.experimental.pallas import tpu as pltpu
from jax.sharding import PartitionSpec as P

MESH = pl.DeviceIdType.MESH
LANES = 128
ROW_TILE = 16


def round_up(value, step):
    return -(-value // step) * step


def unit_rms(values):
    return values * lax.rsqrt(jnp.mean(values * values, axis=-1, keepdims=True) + 1e-06)


def dot(left, right, dims=((1,), (0,))):
    return lax.dot_general(left, right, (dims, ((), ())), preferred_element_type=jnp.float32)


def steps(index, size, count):
    return sum(((index >= m * size).astype(jnp.int32) for m in range(1, count)), jnp.zeros_like(index))


def split_rows(values, main_ref, tail_ref, first, last):
    count, main, _ = main_ref.shape
    main_ref[:, :, first:last] = values[: count * main].reshape(count, main, last - first).astype(main_ref.dtype)
    if tail_ref.shape[0]:
        tail = tail_ref.shape[1]
        for at in range(count):
            here = count * main + at * tail
            tail_ref[at, :, first:last] = values[here : here + tail].astype(tail_ref.dtype)


def join_rows(main_ref, tail_ref, first, last):
    count, main, _ = main_ref.shape
    parts = [main_ref[:, :, first:last].astype(jnp.float32).reshape(count * main, last - first)]
    parts += [tail_ref[at, :, first:last].astype(jnp.float32) for at in range(tail_ref.shape[0])]
    return jnp.concatenate(parts, axis=0)


def flip(index, mask):
    moved, bit = index, 1
    while bit <= mask:
        if mask & bit:
            moved = moved + bit * (1 - 2 * ((index // bit) % 2))
        bit *= 2
    return moved


def one_hot(mask):
    return jnp.where(mask, 1.0, 0.0).astype(jnp.bfloat16)


def layer_kernel(
    sizes,
    tokens_any,
    listed_any,
    expert_any,
    gain_any,
    select_any,
    router_any,
    qkv_any,
    wout_any,
    gate_any,
    up_any,
    down_any,
    out_ref,
    tokens_ref,
    listed_ref,
    expert_ref,
    gain_ref,
    select_ref,
    router_ref,
    pick,
    head,
    keyval,
    contrib,
    returned,
    pick_tail,
    head_tail,
    contrib_tail,
    returned_tail,
    residual_ref,
    outbound,
    arrived,
    leaving,
    back,
    qkv,
    wout,
    gate_w,
    up_w,
    down_w,
    small_sem,
    local_sem,
    a_send,
    a_recv,
    w_send,
    w_recv,
    b_send,
    b_recv,
    c_send,
    c_recv,
    d_send,
    d_recv,
    e_send,
    e_recv,
):
    n_tok, n_qp, n_rep, main, tail, capacity, groups = sizes
    n_head, n_exp = n_tok * n_rep, n_tok * n_qp
    block_rows, width = tokens_ref.shape
    head_width = wout.shape[0]
    main_rows, rows = n_head * main, n_head * (main + tail)
    all_tokens = float(n_exp * n_rep * block_rows)
    tok, qp, rep = lax.axis_index("tok"), lax.axis_index("qp"), lax.axis_index("rep")
    my_head = tok * n_rep + rep
    my_exp = tok * n_qp + qp

    def head_device(index):
        return {"tok": index // n_rep, "rep": index % n_rep}

    def exp_device(index):
        return {"tok": index // n_qp, "qp": index % n_qp}

    def remote(src, dst, send, recv, device):
        return pltpu.make_async_remote_copy(
            src_ref=src, dst_ref=dst, send_sem=send, recv_sem=recv, device_id=device, device_id_type=MESH
        )

    barrier = pltpu.get_barrier_semaphore()
    for k in range(1, n_head):
        pl.semaphore_signal(barrier, inc=1, device_id=head_device((my_head + k) % n_head), device_id_type=MESH)
    for k in range(1, n_exp):
        pl.semaphore_signal(barrier, inc=1, device_id=exp_device((my_exp + k) % n_exp), device_id_type=MESH)

    small = [
        pltpu.make_async_copy(src, dst, small_sem.at[at])
        for at, (src, dst) in enumerate(
            (
                (listed_any, listed_ref),
                (tokens_any, tokens_ref),
                (expert_any, expert_ref),
                (gain_any, gain_ref),
                (select_any, select_ref),
                (router_any, router_ref),
            )
        )
    ]
    for copy in small:
        copy.start()
    local = [
        pltpu.make_async_copy(qkv_any.at[0], qkv, local_sem.at[0]),
        pltpu.make_async_copy(wout_any.at[0], wout, local_sem.at[1]),
        pltpu.make_async_copy(gate_any.at[0], gate_w.at[rep], local_sem.at[2]),
        pltpu.make_async_copy(up_any.at[0], up_w.at[rep], local_sem.at[3]),
        pltpu.make_async_copy(down_any.at[0], down_w.at[rep], local_sem.at[4]),
    ]
    for copy in local:
        copy.start()

    row_index = lax.broadcasted_iota(jnp.int32, (rows, 1), 0)
    block_of = steps(row_index, main, n_head)
    within = row_index - block_of * main
    if tail:
        tail_index = row_index - main_rows
        tail_block = steps(tail_index, tail, n_head)
        block_of = jnp.where(tail_index >= 0, tail_block, block_of)
        within = jnp.where(tail_index >= 0, main + tail_index - tail_block * tail, within)
    slot_count = listed_ref.shape[2]
    small[0].wait()
    spread = one_hot(block_of == lax.broadcasted_iota(jnp.int32, (rows, n_head), 1))
    listed_rows = dot(spread, listed_ref[0].astype(jnp.float32).astype(jnp.bfloat16))
    at_slot = within == lax.broadcasted_iota(jnp.int32, (rows, slot_count), 1)
    place = jnp.sum(jnp.where(at_slot, listed_rows, 0.0), axis=1, keepdims=True)
    place = jnp.where(within < slot_count, place, -1.0)
    lane_index = lax.broadcasted_iota(jnp.int32, (rows, block_rows), 1)
    chosen = one_hot(place.astype(jnp.int32) == lane_index)
    small[1].wait()
    picked = dot(chosen, tokens_ref[...])
    split_rows(picked, pick, pick_tail, 0, width)
    split_rows(jnp.broadcast_to(place, (rows, LANES)), pick, pick_tail, width, width + LANES)

    pl.semaphore_wait(barrier, n_head - 1 + n_exp - 1)

    sends = []

    def start(copy):
        copy.start()
        sends.append(copy)

    for k in range(1, n_head):
        to = flip(my_head, n_head - k)
        start(remote(pick.at[to], head.at[my_head], a_send.at[k], a_recv.at[k], head_device(to)))
        if tail:
            start(remote(pick_tail.at[to], head_tail.at[my_head], a_send.at[n_head + k], a_recv.at[n_head + k], head_device(to)))
    for k in range(1, n_rep):
        to = {"rep": (rep + k) % n_rep}
        for at, (src, dst) in enumerate(((gate_any, gate_w), (up_any, up_w), (down_any, down_w))):
            start(remote(src.at[0], dst.at[rep], w_send.at[k, at], w_recv.at[k, at], to))
    head[my_head] = pick[my_head]
    if tail:
        head_tail[my_head] = pick_tail[my_head]

    for copy in small[2:]:
        copy.wait()
    expert = expert_ref[...]
    named = expert == lax.broadcasted_iota(jnp.int32, (n_exp, block_rows), 0)
    earlier = lax.broadcasted_iota(jnp.int32, (block_rows, block_rows), 0) <= lax.broadcasted_iota(
        jnp.int32, (block_rows, block_rows), 1
    )
    running = dot(one_hot(named), one_hot(earlier))
    slot_of = jnp.sum(jnp.where(named, running, 0.0), axis=0, keepdims=True) - 1.0
    slot_key = expert * capacity + slot_of.astype(jnp.int32)
    seat = one_hot(slot_key == lax.broadcasted_iota(jnp.int32, (n_exp * capacity, block_rows), 0))

    local[0].wait()
    local[1].wait()
    for k in range(1, n_head):
        source = flip(my_head, n_head - k)
        remote(pick.at[source], head.at[source], a_send.at[k], a_recv.at[k], head_device(source)).wait_recv()
        if tail:
            remote(pick_tail.at[source], head_tail.at[source], a_send.at[n_head + k], a_recv.at[n_head + k], head_device(source)).wait_recv()

    head_rows = join_rows(head, head_tail, 0, width).astype(jnp.bfloat16)
    projected = dot(head_rows, qkv[...])
    queries = unit_rms(projected[:, :head_width]).astype(jnp.bfloat16)
    keyval[qp, :, :head_width] = unit_rms(projected[:, head_width : 2 * head_width]).astype(jnp.bfloat16)
    keyval[qp, :, head_width : 2 * head_width] = projected[:, 2 * head_width :].astype(jnp.bfloat16)
    keyval[qp, :, 2 * head_width :] = join_rows(head, head_tail, width, width + LANES).astype(jnp.bfloat16)
    for k in range(1, n_qp):
        start(remote(keyval.at[qp], keyval.at[qp], b_send.at[k], b_recv.at[k], {"qp": (qp + k) % n_qp}))

    base_block = block_of + steps(block_of, n_rep, n_tok) * ((n_qp - 1) * n_rep)

    def positions(source):
        inside = keyval[source, :, 2 * head_width :].astype(jnp.float32)
        base = ((base_block + source * n_rep) * block_rows).astype(jnp.float32)
        return jnp.where(inside >= 0.0, base + inside, all_tokens)

    query_places = positions(qp)[:, :1]
    head_gate = jax.nn.sigmoid(
        jnp.sum(head_rows.astype(jnp.float32) * select_ref[...].astype(jnp.float32), axis=1, keepdims=True)
    )
    head_gate = jnp.where(query_places < all_tokens, head_gate, 0.0)
    numerator = jnp.zeros((rows, head_width), jnp.float32)
    denominator = jnp.zeros((rows, 1), jnp.float32)
    for k in range(n_qp):
        source = (qp + n_qp - k) % n_qp
        if k:
            remote(keyval.at[source], keyval.at[source], b_send.at[k], b_recv.at[k], {"qp": source}).wait_recv()
        key_places = jnp.transpose(positions(source))[:1]
        scores = dot(queries, keyval[source, :, :head_width], ((1,), (1,))) * head_width**-0.5
        weights = jnp.where(key_places <= query_places, jnp.exp(scores), 0.0)
        denominator = denominator + jnp.sum(weights, axis=1, keepdims=True)
        numerator = numerator + dot(
            weights.astype(jnp.bfloat16), keyval[source, :, head_width : 2 * head_width]
        )
    attended = (numerator / denominator).astype(jnp.bfloat16)
    split_rows(dot(attended, wout[...]) * head_gate, contrib, contrib_tail, 0, width)
    for k in range(1, n_head):
        to = flip(my_head, n_head - k)
        start(remote(contrib.at[to], returned.at[my_head], c_send.at[k], c_recv.at[k], head_device(to)))
        if tail:
            start(remote(contrib_tail.at[to], returned_tail.at[my_head], c_send.at[n_head + k], c_recv.at[n_head + k], head_device(to)))
    returned[my_head] = contrib[my_head]
    if tail:
        returned_tail[my_head] = contrib_tail[my_head]
    for k in range(1, n_head):
        source = flip(my_head, n_head - k)
        remote(contrib.at[source], returned.at[source], c_send.at[k], c_recv.at[k], head_device(source)).wait_recv()
        if tail:
            remote(contrib_tail.at[source], returned_tail.at[source], c_send.at[n_head + k], c_recv.at[n_head + k], head_device(source)).wait_recv()

    attention = dot(chosen, join_rows(returned, returned_tail, 0, width).astype(jnp.bfloat16), ((0,), (0,)))
    residual = tokens_ref[...].astype(jnp.float32) + attention
    residual_ref[...] = residual
    normed = (unit_rms(residual) * gain_ref[...].astype(jnp.float32).reshape(1, width)).astype(jnp.bfloat16)
    outbound[...] = dot(seat, normed).astype(jnp.bfloat16).reshape(n_exp, capacity, width)
    for k in range(n_exp - 1):
        to = flip(my_exp, n_exp - 1 - k)
        start(remote(outbound.at[to], arrived.at[k], d_send.at[k], d_recv.at[k], exp_device(to)))
    arrived[n_exp - 1] = outbound[my_exp]

    for copy in local[2:]:
        copy.wait()
    for k in range(1, n_rep):
        source = (rep + n_rep - k) % n_rep
        for at, (src, dst) in enumerate(((gate_any, gate_w), (up_any, up_w), (down_any, down_w))):
            remote(src.at[0], dst.at[source], w_send.at[k, at], w_recv.at[k, at], {"rep": source}).wait_recv()

    group = n_exp // groups
    for first in range(0, n_exp, group):
        for k in range(first, min(first + group, n_exp - 1)):
            source = flip(my_exp, n_exp - 1 - k)
            remote(outbound.at[source], arrived.at[k], d_send.at[k], d_recv.at[k], exp_device(source)).wait_recv()
        flat = arrived[first : first + group].reshape(group * capacity, width)
        total = jnp.zeros((group * capacity, width), jnp.float32)
        for part in range(n_rep):
            hidden = (jax.nn.silu(dot(flat, gate_w[part])) * dot(flat, up_w[part])).astype(jnp.bfloat16)
            total = total + dot(hidden, down_w[part])
        router_gate = jax.nn.sigmoid(
            jnp.sum(flat.astype(jnp.float32) * router_ref[...].astype(jnp.float32), axis=1, keepdims=True)
        )
        leaving[first : first + group] = (total * router_gate).astype(jnp.bfloat16).reshape(group, capacity, width)
        for k in range(first, min(first + group, n_exp - 1)):
            source = flip(my_exp, n_exp - 1 - k)
            start(remote(leaving.at[k], back.at[my_exp], e_send.at[k], e_recv.at[k], exp_device(source)))
    back[my_exp] = leaving[n_exp - 1]
    for k in range(n_exp - 1):
        owner = flip(my_exp, n_exp - 1 - k)
        remote(leaving.at[k], back.at[owner], e_send.at[k], e_recv.at[k], exp_device(owner)).wait_recv()
    routed = dot(seat, back[...].reshape(n_exp * capacity, width), ((0,), (0,)))
    out_ref[...] = (residual_ref[...] + routed).astype(out_ref.dtype)
    for copy in sends:
        copy.wait_send()


def local(
    mesh_sizes, tokens, listed, w_qkv, w_out, w_select, norm_gain, expert_id, router, w_gate, w_up, w_down
):
    n_tok, n_qp, n_rep = mesh_sizes
    n_head, n_exp = n_tok * n_rep, n_tok * n_qp
    block_rows, width = tokens.shape
    assert n_head & (n_head - 1) == 0 and n_exp & (n_exp - 1) == 0
    slot_count = listed.shape[2]
    head_width = w_out.shape[1]
    assert listed.shape[1] == n_head and w_out.shape[0] == 1 and w_gate.shape[0] == 1
    assert block_rows <= 2 * LANES
    main = slot_count // 8 * 8
    tail = 1 << (slot_count - main - 1).bit_length() if slot_count > main else 0
    assert main
    slots = main + tail
    capacity = round_up(max(2, 2 * block_rows // n_exp), ROW_TILE)
    groups = n_tok if n_exp % n_tok == 0 else 1
    groups = min(groups, 4)
    rows = n_head * slots
    bf16 = jnp.bfloat16
    dma = pltpu.SemaphoreType.DMA
    vmem, anywhere = pl.BlockSpec(memory_space=pltpu.VMEM), pl.BlockSpec(memory_space=pltpu.HBM)
    hidden = w_gate.shape[2]
    tail_count = n_head if tail else 0
    small = [tokens, listed, expert_id.reshape(1, -1), norm_gain, w_select, router]
    scratch = [pltpu.VMEM(array.shape, array.dtype) for array in small]
    scratch += [
        pltpu.VMEM((n_head, main, width + LANES), bf16),
        pltpu.VMEM((n_head, main, width + LANES), bf16),
        pltpu.VMEM((n_qp, rows, 2 * head_width + LANES), bf16),
        pltpu.VMEM((n_head, main, width), bf16),
        pltpu.VMEM((n_head, main, width), bf16),
        pltpu.VMEM((tail_count, tail, width + LANES), bf16),
        pltpu.VMEM((tail_count, tail, width + LANES), bf16),
        pltpu.VMEM((tail_count, tail, width), bf16),
        pltpu.VMEM((tail_count, tail, width), bf16),
        pltpu.VMEM((block_rows, width), jnp.float32),
        pltpu.VMEM((n_exp, capacity, width), bf16),
        pltpu.VMEM((n_exp, capacity, width), bf16),
        pltpu.VMEM((n_exp, capacity, width), bf16),
        pltpu.VMEM((n_exp, capacity, width), bf16),
        pltpu.VMEM(w_qkv.shape[1:], bf16),
        pltpu.VMEM(w_out.shape[1:], bf16),
        pltpu.VMEM((n_rep, width, hidden), bf16),
        pltpu.VMEM((n_rep, width, hidden), bf16),
        pltpu.VMEM((n_rep, hidden, width), bf16),
    ]
    semaphores = [(len(small),), (5,), (2 * n_head,), (2 * n_head,), (n_rep, 3), (n_rep, 3), (n_qp,), (n_qp,)]
    semaphores += [(2 * n_head,), (2 * n_head,), (n_exp,), (n_exp,), (n_exp,), (n_exp,)]
    return pl.pallas_call(
        functools.partial(layer_kernel, (n_tok, n_qp, n_rep, main, tail, capacity, groups)),
        out_shape=pltpu.VMEM((block_rows, width), bf16),
        in_specs=[anywhere] * 11,
        out_specs=vmem,
        scratch_shapes=scratch + [dma(shape) for shape in semaphores],
        compiler_params=pltpu.CompilerParams(
            collective_id=0, has_side_effects=True, vmem_limit_bytes=60 << 20
        ),
    )(
        *small,
        w_qkv,
        w_out,
        w_gate,
        w_up,
        w_down,
    )


def solution(mesh):
    in_specs = (
        P(("group", "tok", "qp", "rep"), None),
        P(("group", "tok", "qp", "rep"), None, None),
        P(("tok", "rep"), None, None),
        P(("tok", "rep"), None, None),
        P(("tok", "rep"), None),
        P(),
        P(("group", "tok", "qp", "rep"), None),
        P(("tok", "qp"), None),
        P(("tok", "qp"), None, "rep"),
        P(("tok", "qp"), None, "rep"),
        P(("tok", "qp"), "rep", None),
    )
    out_specs = P(("group", "tok", "qp", "rep"), None)
    sizes = (mesh.shape["tok"], mesh.shape["qp"], mesh.shape["rep"])
    return jax.shard_map(
        functools.partial(local, sizes), mesh=mesh, in_specs=in_specs, out_specs=out_specs, check_vma=False
    )
```

```python
import functools
import jax
import jax.numpy as jnp
from jax import lax
from jax.experimental import pallas as pl
from jax.experimental.pallas import tpu as pltpu
from jax.sharding import PartitionSpec as P

MESH = pl.DeviceIdType.MESH
LANES = 128
ROW_TILE = 16


def round_up(value, step):
    return -(-value // step) * step


def unit_rms(values):
    return values * lax.rsqrt(jnp.mean(values * values, axis=-1, keepdims=True) + 1e-06)


def dot(left, right, dims=((1,), (0,))):
    return lax.dot_general(left, right, (dims, ((), ())), preferred_element_type=jnp.float32)


def steps(index, size, count):
    return sum(((index >= m * size).astype(jnp.int32) for m in range(1, count)), jnp.zeros_like(index))


def split_rows(values, main_ref, tail_ref, first, last):
    count, main, _ = main_ref.shape
    main_ref[:, :, first:last] = values[: count * main].reshape(count, main, last - first).astype(main_ref.dtype)
    if tail_ref.shape[0]:
        tail = tail_ref.shape[1]
        for at in range(count):
            here = count * main + at * tail
            tail_ref[at, :, first:last] = values[here : here + tail].astype(tail_ref.dtype)


def join_rows(main_ref, tail_ref, first, last):
    count, main, _ = main_ref.shape
    parts = [main_ref[:, :, first:last].astype(jnp.float32).reshape(count * main, last - first)]
    parts += [tail_ref[at, :, first:last].astype(jnp.float32) for at in range(tail_ref.shape[0])]
    return jnp.concatenate(parts, axis=0)


def flip(index, mask):
    moved, bit = index, 1
    while bit <= mask:
        if mask & bit:
            moved = moved + bit * (1 - 2 * ((index // bit) % 2))
        bit *= 2
    return moved


def one_hot(mask):
    return jnp.where(mask, 1.0, 0.0).astype(jnp.bfloat16)


def layer_kernel(
    sizes,
    tokens_any,
    listed_any,
    expert_any,
    gain_any,
    select_any,
    router_any,
    qkv_any,
    wout_any,
    gate_any,
    up_any,
    down_any,
    out_ref,
    tokens_ref,
    listed_ref,
    expert_ref,
    gain_ref,
    select_ref,
    router_ref,
    pick,
    head,
    keyval,
    contrib,
    returned,
    pick_tail,
    head_tail,
    contrib_tail,
    returned_tail,
    residual_ref,
    outbound,
    outbound_early,
    over_out,
    over_in,
    arrived,
    leaving,
    back,
    qkv,
    wout,
    gate_w,
    up_w,
    down_w,
    small_sem,
    local_sem,
    a_send,
    a_recv,
    w_send,
    w_recv,
    b_send,
    b_recv,
    c_send,
    c_recv,
    d_send,
    d_recv,
    f_send,
    f_recv,
    o_send,
    o_recv,
    e_send,
    e_recv,
):
    n_tok, n_qp, n_rep, main, tail, capacity, early, groups = sizes
    n_head, n_exp = n_tok * n_rep, n_tok * n_qp
    block_rows, width = tokens_ref.shape
    head_width = wout.shape[0]
    main_rows, rows = n_head * main, n_head * (main + tail)
    all_tokens = float(n_exp * n_rep * block_rows)
    tok, qp, rep = lax.axis_index("tok"), lax.axis_index("qp"), lax.axis_index("rep")
    my_head = tok * n_rep + rep
    my_exp = tok * n_qp + qp

    def head_device(index):
        return {"tok": index // n_rep, "rep": index % n_rep}

    def exp_device(index):
        return {"tok": index // n_qp, "qp": index % n_qp}

    def remote(src, dst, send, recv, device):
        return pltpu.make_async_remote_copy(
            src_ref=src, dst_ref=dst, send_sem=send, recv_sem=recv, device_id=device, device_id_type=MESH
        )

    barrier = pltpu.get_barrier_semaphore()
    for k in range(1, n_head):
        pl.semaphore_signal(barrier, inc=1, device_id=head_device((my_head + k) % n_head), device_id_type=MESH)
    for k in range(1, n_exp):
        pl.semaphore_signal(barrier, inc=1, device_id=exp_device((my_exp + k) % n_exp), device_id_type=MESH)

    small = [
        pltpu.make_async_copy(src, dst, small_sem.at[at])
        for at, (src, dst) in enumerate(
            (
                (listed_any, listed_ref),
                (tokens_any, tokens_ref),
                (expert_any, expert_ref),
                (gain_any, gain_ref),
                (select_any, select_ref),
                (router_any, router_ref),
            )
        )
    ]
    for copy in small:
        copy.start()
    local = [
        pltpu.make_async_copy(qkv_any.at[0], qkv, local_sem.at[0]),
        pltpu.make_async_copy(wout_any.at[0], wout, local_sem.at[1]),
        pltpu.make_async_copy(gate_any.at[0], gate_w.at[rep], local_sem.at[2]),
        pltpu.make_async_copy(up_any.at[0], up_w.at[rep], local_sem.at[3]),
        pltpu.make_async_copy(down_any.at[0], down_w.at[rep], local_sem.at[4]),
    ]
    for copy in local:
        copy.start()

    row_index = lax.broadcasted_iota(jnp.int32, (rows, 1), 0)
    block_of = steps(row_index, main, n_head)
    within = row_index - block_of * main
    if tail:
        tail_index = row_index - main_rows
        tail_block = steps(tail_index, tail, n_head)
        block_of = jnp.where(tail_index >= 0, tail_block, block_of)
        within = jnp.where(tail_index >= 0, main + tail_index - tail_block * tail, within)
    slot_count = listed_ref.shape[2]
    small[0].wait()
    spread = one_hot(block_of == lax.broadcasted_iota(jnp.int32, (rows, n_head), 1))
    listed_rows = dot(spread, listed_ref[0].astype(jnp.float32).astype(jnp.bfloat16))
    at_slot = within == lax.broadcasted_iota(jnp.int32, (rows, slot_count), 1)
    place = jnp.sum(jnp.where(at_slot, listed_rows, 0.0), axis=1, keepdims=True)
    place = jnp.where(within < slot_count, place, -1.0)
    lane_index = lax.broadcasted_iota(jnp.int32, (rows, block_rows), 1)
    chosen = one_hot(place.astype(jnp.int32) == lane_index)
    small[1].wait()
    picked = dot(chosen, tokens_ref[...])
    split_rows(picked, pick, pick_tail, 0, width)
    split_rows(jnp.broadcast_to(place, (rows, LANES)), pick, pick_tail, width, width + LANES)

    for copy in small[2:]:
        copy.wait()
    expert = expert_ref[...]
    late = capacity - early
    is_listed = jnp.sum(chosen.astype(jnp.float32), axis=0, keepdims=True) > 0.0
    named = expert == lax.broadcasted_iota(jnp.int32, (n_exp, block_rows), 0)
    named_listed = jnp.where(named & is_listed, 1.0, 0.0)
    named_plain = jnp.where(named, 1.0, 0.0) - named_listed
    earlier = one_hot(
        lax.broadcasted_iota(jnp.int32, (block_rows, block_rows), 0)
        <= lax.broadcasted_iota(jnp.int32, (block_rows, block_rows), 1)
    )
    listed_rank = dot(named_listed.astype(jnp.bfloat16), earlier) - 1.0
    plain_rank = dot(named_plain.astype(jnp.bfloat16), earlier) - 1.0
    listed_count = jnp.sum(named_listed, axis=1, keepdims=True)
    over = jnp.maximum(listed_count - late, 0.0)
    below = one_hot(
        lax.broadcasted_iota(jnp.int32, (n_exp, n_exp), 1) < lax.broadcasted_iota(jnp.int32, (n_exp, n_exp), 0)
    )
    over_first = dot(below, jnp.broadcast_to(over, (n_exp, block_rows)).astype(jnp.bfloat16))
    listed_slot = jnp.where(listed_rank < late, early + listed_rank, over_first + listed_rank - late)
    plain_slot = jnp.where((plain_rank < over_first) | (over < 0.5), plain_rank, plain_rank + over)
    plain_slot = jnp.where(plain_slot < early, plain_slot, plain_rank + jnp.minimum(listed_count, late))
    slot_of = jnp.sum(named_listed * listed_slot + named_plain * plain_slot, axis=0, keepdims=True).astype(jnp.int32)

    def seats(size, count, kept):
        key = jnp.where(kept, expert * count + slot_of - size, -1)
        return one_hot(key == lax.broadcasted_iota(jnp.int32, (n_exp * count, block_rows), 0))

    seat = seats(0, capacity, slot_of >= 0)
    late_seat = seats(early, late, slot_of >= early) if early else seat
    gain = gain_ref[...].astype(jnp.float32).reshape(1, width)
    if early:
        plain = (unit_rms(tokens_ref[...].astype(jnp.float32)) * gain).astype(jnp.bfloat16)
        early_seat = seats(0, early, (slot_of < early) & jnp.logical_not(is_listed))
        outbound_early[...] = dot(early_seat, plain).astype(jnp.bfloat16).reshape(n_exp, early, width)
        over_seat = (slot_of == lax.broadcasted_iota(jnp.int32, (early, block_rows), 0)) & is_listed
        over_name = jnp.sum(jnp.where(over_seat, (expert + 1).astype(jnp.float32), 0.0), axis=1, keepdims=True)

    pl.semaphore_wait(barrier, n_head - 1 + n_exp - 1)

    sends = []

    def start(copy):
        copy.start()
        sends.append(copy)

    for k in range(1, n_head):
        to = flip(my_head, n_head - k)
        start(remote(pick.at[to], head.at[my_head], a_send.at[k], a_recv.at[k], head_device(to)))
        if tail:
            start(remote(pick_tail.at[to], head_tail.at[my_head], a_send.at[n_head + k], a_recv.at[n_head + k], head_device(to)))
    a_sends = sends[:]
    sends.clear()
    for k in range(1, n_rep):
        to = {"rep": (rep + k) % n_rep}
        for at, (src, dst) in enumerate(((gate_any, gate_w), (up_any, up_w), (down_any, down_w))):
            start(remote(src.at[0], dst.at[rep], w_send.at[k, at], w_recv.at[k, at], to))
    head[my_head] = pick[my_head]
    if tail:
        head_tail[my_head] = pick_tail[my_head]

    for copy in a_sends:
        copy.wait_send()
    if early:
        for k in [0]:
            to = flip(my_exp, n_exp - 1 - k)
            start(remote(outbound_early.at[to], arrived.at[k, pl.ds(0, early)], f_send.at[k], f_recv.at[k], exp_device(to)))
    local[0].wait()
    local[1].wait()
    for k in range(1, n_head):
        source = flip(my_head, n_head - k)
        remote(pick.at[source], head.at[source], a_send.at[k], a_recv.at[k], head_device(source)).wait_recv()
        if tail:
            remote(pick_tail.at[source], head_tail.at[source], a_send.at[n_head + k], a_recv.at[n_head + k], head_device(source)).wait_recv()

    if early:
        for k in [1, 2, 3, 4, 5, 6]:
            to = flip(my_exp, n_exp - 1 - k)
            start(remote(outbound_early.at[to], arrived.at[k, pl.ds(0, early)], f_send.at[k], f_recv.at[k], exp_device(to)))
        arrived[n_exp - 1, :early] = outbound_early[my_exp]
    head_rows = join_rows(head, head_tail, 0, width).astype(jnp.bfloat16)
    projected = dot(head_rows, qkv[...])
    queries = unit_rms(projected[:, :head_width]).astype(jnp.bfloat16)
    keyval[qp, :, :head_width] = unit_rms(projected[:, head_width : 2 * head_width]).astype(jnp.bfloat16)
    keyval[qp, :, head_width : 2 * head_width] = projected[:, 2 * head_width :].astype(jnp.bfloat16)
    keyval[qp, :, 2 * head_width :] = join_rows(head, head_tail, width, width + LANES).astype(jnp.bfloat16)
    for k in range(1, n_qp):
        start(remote(keyval.at[qp], keyval.at[qp], b_send.at[k], b_recv.at[k], {"qp": (qp + k) % n_qp}))

    base_block = block_of + steps(block_of, n_rep, n_tok) * ((n_qp - 1) * n_rep)

    def positions(source):
        inside = keyval[source, :, 2 * head_width :].astype(jnp.float32)
        base = ((base_block + source * n_rep) * block_rows).astype(jnp.float32)
        return jnp.where(inside >= 0.0, base + inside, all_tokens)

    query_places = positions(qp)[:, :1]
    head_gate = jax.nn.sigmoid(
        jnp.sum(head_rows.astype(jnp.float32) * select_ref[...].astype(jnp.float32), axis=1, keepdims=True)
    )
    head_gate = jnp.where(query_places < all_tokens, head_gate, 0.0)
    numerator = jnp.zeros((rows, head_width), jnp.float32)
    denominator = jnp.zeros((rows, 1), jnp.float32)
    for k in range(n_qp):
        source = (qp + n_qp - k) % n_qp
        if k:
            remote(keyval.at[source], keyval.at[source], b_send.at[k], b_recv.at[k], {"qp": source}).wait_recv()
        key_places = jnp.transpose(positions(source))[:1]
        scores = dot(queries, keyval[source, :, :head_width], ((1,), (1,))) * head_width**-0.5
        weights = jnp.where(key_places <= query_places, jnp.exp(scores), 0.0)
        denominator = denominator + jnp.sum(weights, axis=1, keepdims=True)
        numerator = numerator + dot(
            weights.astype(jnp.bfloat16), keyval[source, :, head_width : 2 * head_width]
        )
    attended = (numerator / denominator).astype(jnp.bfloat16)
    split_rows(dot(attended, wout[...]) * head_gate, contrib, contrib_tail, 0, width)
    for k in range(1, n_head):
        to = flip(my_head, n_head - k)
        start(remote(contrib.at[to], returned.at[my_head], c_send.at[k], c_recv.at[k], head_device(to)))
        if tail:
            start(remote(contrib_tail.at[to], returned_tail.at[my_head], c_send.at[n_head + k], c_recv.at[n_head + k], head_device(to)))
    returned[my_head] = contrib[my_head]
    if tail:
        returned_tail[my_head] = contrib_tail[my_head]
    for k in range(1, n_head):
        source = flip(my_head, n_head - k)
        remote(contrib.at[source], returned.at[source], c_send.at[k], c_recv.at[k], head_device(source)).wait_recv()
        if tail:
            remote(contrib_tail.at[source], returned_tail.at[source], c_send.at[n_head + k], c_recv.at[n_head + k], head_device(source)).wait_recv()

    attention = dot(chosen, join_rows(returned, returned_tail, 0, width).astype(jnp.bfloat16), ((0,), (0,)))
    residual = tokens_ref[...].astype(jnp.float32) + attention
    residual_ref[...] = residual
    normed = (unit_rms(residual) * gain).astype(jnp.bfloat16)
    half = n_exp // 2
    partner = flip(my_exp, half)
    if early:
        over_out[:, :width] = dot(one_hot(over_seat), normed).astype(jnp.bfloat16)
        over_out[:, width:] = jnp.broadcast_to(over_name, (early, LANES)).astype(jnp.bfloat16)
        for m in [half, *range(1, half)]:
            to = flip(my_exp, m)
            start(remote(over_out, over_in.at[my_exp], o_send.at[m], o_recv.at[m], exp_device(to)))
        over_in[my_exp] = over_out[...]
    outbound[...] = dot(late_seat, normed).astype(jnp.bfloat16).reshape(n_exp, late, width)

    def late_part(k):
        return arrived.at[k, pl.ds(early, late)]

    for k in range(n_exp - 1):
        to = flip(my_exp, n_exp - 1 - k)
        start(remote(outbound.at[to], late_part(k), d_send.at[k], d_recv.at[k], exp_device(to)))
    arrived[n_exp - 1, early:] = outbound[my_exp]
    if early:
        remote(over_out, over_in.at[partner], o_send.at[half], o_recv.at[half], exp_device(partner)).wait_recv()
        for m in range(1, half):
            to = flip(my_exp, m)
            start(remote(over_in.at[partner], over_in.at[partner], o_send.at[half + m], o_recv.at[half + m], exp_device(to)))

    for copy in local[2:]:
        copy.wait()
    for k in range(1, n_rep):
        source = (rep + n_rep - k) % n_rep
        for at, (src, dst) in enumerate(((gate_any, gate_w), (up_any, up_w), (down_any, down_w))):
            remote(src.at[0], dst.at[source], w_send.at[k, at], w_recv.at[k, at], {"rep": source}).wait_recv()

    if early:
        for m in range(1, half):
            beside = flip(my_exp, m)
            beyond = flip(beside, half)
            remote(over_out, over_in.at[beside], o_send.at[m], o_recv.at[m], exp_device(beside)).wait_recv()
            remote(over_in.at[beyond], over_in.at[beyond], o_send.at[half + m], o_recv.at[half + m], exp_device(beside)).wait_recv()

    group = n_exp // groups
    for first in range(0, n_exp, group):
        for k in range(first, min(first + group, n_exp - 1)):
            source = flip(my_exp, n_exp - 1 - k)
            if early:
                remote(outbound_early.at[source], arrived.at[k, pl.ds(0, early)], f_send.at[k], f_recv.at[k], exp_device(source)).wait_recv()
            remote(outbound.at[source], late_part(k), d_send.at[k], d_recv.at[k], exp_device(source)).wait_recv()
        for k in range(first, first + group if early else first):
            block = flip(my_exp, n_exp - 1 - k)
            extra = over_in[block].astype(jnp.float32)
            here = arrived[k, :early].astype(jnp.float32)
            taken = extra[:, width : width + 1] == (my_exp + 1).astype(jnp.float32)
            arrived[k, :early] = jnp.where(taken, extra[:, :width], here).astype(jnp.bfloat16)
        flat = arrived[first : first + group].reshape(group * capacity, width)
        total = jnp.zeros((group * capacity, width), jnp.float32)
        for part in range(n_rep):
            hidden = (jax.nn.silu(dot(flat, gate_w[part])) * dot(flat, up_w[part])).astype(jnp.bfloat16)
            total = total + dot(hidden, down_w[part])
        router_gate = jax.nn.sigmoid(
            jnp.sum(flat.astype(jnp.float32) * router_ref[...].astype(jnp.float32), axis=1, keepdims=True)
        )
        leaving[first : first + group] = (total * router_gate).astype(jnp.bfloat16).reshape(group, capacity, width)
        for k in range(first, min(first + group, n_exp - 1)):
            source = flip(my_exp, n_exp - 1 - k)
            start(remote(leaving.at[k], back.at[my_exp], e_send.at[k], e_recv.at[k], exp_device(source)))
    back[my_exp] = leaving[n_exp - 1]
    for k in range(n_exp - 1):
        owner = flip(my_exp, n_exp - 1 - k)
        remote(leaving.at[k], back.at[owner], e_send.at[k], e_recv.at[k], exp_device(owner)).wait_recv()
    routed = dot(seat, back[...].reshape(n_exp * capacity, width), ((0,), (0,)))
    out_ref[...] = (residual_ref[...] + routed).astype(out_ref.dtype)
    for copy in sends:
        copy.wait_send()


def local(
    mesh_sizes, tokens, listed, w_qkv, w_out, w_select, norm_gain, expert_id, router, w_gate, w_up, w_down
):
    n_tok, n_qp, n_rep = mesh_sizes
    n_head, n_exp = n_tok * n_rep, n_tok * n_qp
    block_rows, width = tokens.shape
    assert n_head & (n_head - 1) == 0 and n_exp & (n_exp - 1) == 0
    slot_count = listed.shape[2]
    head_width = w_out.shape[1]
    assert listed.shape[1] == n_head and w_out.shape[0] == 1 and w_gate.shape[0] == 1
    assert block_rows <= 2 * LANES
    main = slot_count // 8 * 8
    tail = 1 << (slot_count - main - 1).bit_length() if slot_count > main else 0
    assert main
    slots = main + tail
    capacity = round_up(max(2, 2 * block_rows // n_exp), ROW_TILE)
    listed_most = n_head * slot_count
    kept = capacity - ROW_TILE
    most_over = max(min(listed_most, capacity * k) - kept * k for k in range(1, n_exp + 1))
    early = ROW_TILE if n_exp > 1 and kept >= ROW_TILE and most_over <= ROW_TILE else 0
    groups = n_tok if n_exp % n_tok == 0 else 1
    groups = min(groups, 4)
    rows = n_head * slots
    bf16 = jnp.bfloat16
    dma = pltpu.SemaphoreType.DMA
    vmem, anywhere = pl.BlockSpec(memory_space=pltpu.VMEM), pl.BlockSpec(memory_space=pltpu.HBM)
    hidden = w_gate.shape[2]
    tail_count = n_head if tail else 0
    small = [tokens, listed, expert_id.reshape(1, -1), norm_gain, w_select, router]
    scratch = [pltpu.VMEM(array.shape, array.dtype) for array in small]
    scratch += [
        pltpu.VMEM((n_head, main, width + LANES), bf16),
        pltpu.VMEM((n_head, main, width + LANES), bf16),
        pltpu.VMEM((n_qp, rows, 2 * head_width + LANES), bf16),
        pltpu.VMEM((n_head, main, width), bf16),
        pltpu.VMEM((n_head, main, width), bf16),
        pltpu.VMEM((tail_count, tail, width + LANES), bf16),
        pltpu.VMEM((tail_count, tail, width + LANES), bf16),
        pltpu.VMEM((tail_count, tail, width), bf16),
        pltpu.VMEM((tail_count, tail, width), bf16),
        pltpu.VMEM((block_rows, width), jnp.float32),
        pltpu.VMEM((n_exp, capacity - early, width), bf16),
        pltpu.VMEM((n_exp if early else 1, ROW_TILE, width), bf16),
        pltpu.VMEM((ROW_TILE, width + LANES), bf16),
        pltpu.VMEM((n_exp if early else 1, ROW_TILE, width + LANES), bf16),
        pltpu.VMEM((n_exp, capacity, width), bf16),
        pltpu.VMEM((n_exp, capacity, width), bf16),
        pltpu.VMEM((n_exp, capacity, width), bf16),
        pltpu.VMEM(w_qkv.shape[1:], bf16),
        pltpu.VMEM(w_out.shape[1:], bf16),
        pltpu.VMEM((n_rep, width, hidden), bf16),
        pltpu.VMEM((n_rep, width, hidden), bf16),
        pltpu.VMEM((n_rep, hidden, width), bf16),
    ]
    semaphores = [(len(small),), (5,), (2 * n_head,), (2 * n_head,), (n_rep, 3), (n_rep, 3), (n_qp,), (n_qp,)]
    semaphores += [(2 * n_head,), (2 * n_head,), *[(n_exp,)] * 8]
    return pl.pallas_call(
        functools.partial(layer_kernel, (n_tok, n_qp, n_rep, main, tail, capacity, early, groups)),
        out_shape=pltpu.VMEM((block_rows, width), bf16),
        in_specs=[anywhere] * 11,
        out_specs=vmem,
        scratch_shapes=scratch + [dma(shape) for shape in semaphores],
        compiler_params=pltpu.CompilerParams(
            collective_id=0, has_side_effects=True, vmem_limit_bytes=60 << 20
        ),
    )(
        *small,
        w_qkv,
        w_out,
        w_gate,
        w_up,
        w_down,
    )


def solution(mesh):
    in_specs = (
        P(("group", "tok", "qp", "rep"), None),
        P(("group", "tok", "qp", "rep"), None, None),
        P(("tok", "rep"), None, None),
        P(("tok", "rep"), None, None),
        P(("tok", "rep"), None),
        P(),
        P(("group", "tok", "qp", "rep"), None),
        P(("tok", "qp"), None),
        P(("tok", "qp"), None, "rep"),
        P(("tok", "qp"), None, "rep"),
        P(("tok", "qp"), "rep", None),
    )
    out_specs = P(("group", "tok", "qp", "rep"), None)
    sizes = (mesh.shape["tok"], mesh.shape["qp"], mesh.shape["rep"])
    return jax.shard_map(
        functools.partial(local, sizes), mesh=mesh, in_specs=in_specs, out_specs=out_specs, check_vma=False
    )
```

```python
import functools
import jax
import jax.numpy as jnp
from jax import lax
from jax.experimental import pallas as pl
from jax.experimental.pallas import tpu as pltpu
from jax.sharding import PartitionSpec as P

MESH = pl.DeviceIdType.MESH
LANES = 128
ROW_TILE = 16


def round_up(value, step):
    return -(-value // step) * step


def unit_rms(values):
    return values * lax.rsqrt(jnp.mean(values * values, axis=-1, keepdims=True) + 1e-06)


def dot(left, right, dims=((1,), (0,))):
    return lax.dot_general(left, right, (dims, ((), ())), preferred_element_type=jnp.float32)


def steps(index, size, count):
    return sum(((index >= m * size).astype(jnp.int32) for m in range(1, count)), jnp.zeros_like(index))


def split_rows(values, main_ref, tail_ref, first, last):
    count, main, _ = main_ref.shape
    main_ref[:, :, first:last] = values[: count * main].reshape(count, main, last - first).astype(main_ref.dtype)
    if tail_ref.shape[0]:
        tail = tail_ref.shape[1]
        for at in range(count):
            here = count * main + at * tail
            tail_ref[at, :, first:last] = values[here : here + tail].astype(tail_ref.dtype)


def join_rows(main_ref, tail_ref, first, last):
    count, main, _ = main_ref.shape
    parts = [main_ref[:, :, first:last].astype(jnp.float32).reshape(count * main, last - first)]
    parts += [tail_ref[at, :, first:last].astype(jnp.float32) for at in range(tail_ref.shape[0])]
    return jnp.concatenate(parts, axis=0)


def flip(index, mask):
    moved, bit = index, 1
    while bit <= mask:
        if mask & bit:
            moved = moved + bit * (1 - 2 * ((index // bit) % 2))
        bit *= 2
    return moved


def one_hot(mask):
    return jnp.where(mask, 1.0, 0.0).astype(jnp.bfloat16)


def layer_kernel(
    sizes,
    tokens_any,
    listed_any,
    expert_any,
    gain_any,
    select_any,
    router_any,
    qkv_any,
    wout_any,
    gate_any,
    up_any,
    down_any,
    out_ref,
    tokens_ref,
    listed_ref,
    expert_ref,
    gain_ref,
    select_ref,
    router_ref,
    pick,
    head,
    keyval,
    contrib,
    returned,
    pick_tail,
    head_tail,
    contrib_tail,
    returned_tail,
    residual_ref,
    outbound,
    outbound_early,
    over_out,
    over_in,
    arrived,
    leaving,
    back,
    qkv,
    wout,
    gate_w,
    up_w,
    down_w,
    entered,
    small_sem,
    local_sem,
    a_send,
    a_recv,
    w_send,
    w_recv,
    b_send,
    b_recv,
    c_send,
    c_recv,
    d_send,
    d_recv,
    f_send,
    f_recv,
    o_send,
    o_recv,
    e_send,
    e_recv,
):
    n_tok, n_qp, n_rep, main, tail, capacity, early, groups = sizes
    n_head, n_exp = n_tok * n_rep, n_tok * n_qp
    block_rows, width = tokens_ref.shape
    head_width = wout.shape[0]
    main_rows, rows = n_head * main, n_head * (main + tail)
    all_tokens = float(n_exp * n_rep * block_rows)
    tok, qp, rep = lax.axis_index("tok"), lax.axis_index("qp"), lax.axis_index("rep")
    my_head = tok * n_rep + rep
    my_exp = tok * n_qp + qp

    def head_device(index):
        return {"tok": index // n_rep, "rep": index % n_rep}

    def exp_device(index):
        return {"tok": index // n_qp, "qp": index % n_qp}

    def remote(src, dst, send, recv, device):
        return pltpu.make_async_remote_copy(
            src_ref=src, dst_ref=dst, send_sem=send, recv_sem=recv, device_id=device, device_id_type=MESH
        )

    barrier = pltpu.get_barrier_semaphore()
    for k in range(1, n_head):
        pl.semaphore_signal(barrier, inc=1, device_id=head_device((my_head + k) % n_head), device_id_type=MESH)
    for k in range(1, n_qp):
        pl.semaphore_signal(barrier, inc=1, device_id={"qp": (qp + k) % n_qp}, device_id_type=MESH)

    small = [
        pltpu.make_async_copy(src, dst, small_sem.at[at])
        for at, (src, dst) in enumerate(
            (
                (listed_any, listed_ref),
                (tokens_any, tokens_ref),
                (expert_any, expert_ref),
                (gain_any, gain_ref),
                (select_any, select_ref),
                (router_any, router_ref),
            )
        )
    ]
    for copy in small:
        copy.start()
    local = [
        pltpu.make_async_copy(qkv_any.at[0], qkv, local_sem.at[0]),
        pltpu.make_async_copy(wout_any.at[0], wout, local_sem.at[1]),
        pltpu.make_async_copy(gate_any.at[0], gate_w.at[rep], local_sem.at[2]),
        pltpu.make_async_copy(up_any.at[0], up_w.at[rep], local_sem.at[3]),
        pltpu.make_async_copy(down_any.at[0], down_w.at[rep], local_sem.at[4]),
    ]
    for copy in local:
        copy.start()

    row_index = lax.broadcasted_iota(jnp.int32, (rows, 1), 0)
    block_of = steps(row_index, main, n_head)
    within = row_index - block_of * main
    if tail:
        tail_index = row_index - main_rows
        tail_block = steps(tail_index, tail, n_head)
        block_of = jnp.where(tail_index >= 0, tail_block, block_of)
        within = jnp.where(tail_index >= 0, main + tail_index - tail_block * tail, within)
    slot_count = listed_ref.shape[2]
    small[0].wait()
    spread = one_hot(block_of == lax.broadcasted_iota(jnp.int32, (rows, n_head), 1))
    at_slot = within == lax.broadcasted_iota(jnp.int32, (rows, slot_count), 1)

    def places(table):
        of_row = jnp.sum(jnp.where(at_slot, dot(spread, table), 0.0), axis=1, keepdims=True)
        return jnp.where(within < slot_count, of_row, -1.0)

    table = listed_ref[0].astype(jnp.float32)
    place = places(table.astype(jnp.bfloat16))
    lane_index = lax.broadcasted_iota(jnp.int32, (rows, block_rows), 1)
    chosen = one_hot(place.astype(jnp.int32) == lane_index)
    small[1].wait()
    picked = dot(chosen, tokens_ref[...])
    split_rows(picked, pick, pick_tail, 0, width)
    bearer, borne = (pick_tail, head_tail) if tail else (pick, head)
    bearer[:, :, width : width + slot_count] = jnp.broadcast_to(
        table[:, None, :], (n_head, bearer.shape[1], slot_count)
    ).astype(jnp.bfloat16)

    for copy in small[2:]:
        copy.wait()
    expert = expert_ref[...]
    late = capacity - early
    is_listed = jnp.sum(chosen.astype(jnp.float32), axis=0, keepdims=True) > 0.0
    named = expert == lax.broadcasted_iota(jnp.int32, (n_exp, block_rows), 0)
    named_listed = jnp.where(named & is_listed, 1.0, 0.0)
    named_plain = jnp.where(named, 1.0, 0.0) - named_listed
    earlier = one_hot(
        lax.broadcasted_iota(jnp.int32, (block_rows, block_rows), 0)
        <= lax.broadcasted_iota(jnp.int32, (block_rows, block_rows), 1)
    )
    listed_rank = dot(named_listed.astype(jnp.bfloat16), earlier) - 1.0
    plain_rank = dot(named_plain.astype(jnp.bfloat16), earlier) - 1.0
    listed_count = jnp.sum(named_listed, axis=1, keepdims=True)
    over = jnp.maximum(listed_count - late, 0.0)
    below = one_hot(
        lax.broadcasted_iota(jnp.int32, (n_exp, n_exp), 1) < lax.broadcasted_iota(jnp.int32, (n_exp, n_exp), 0)
    )
    over_first = dot(below, jnp.broadcast_to(over, (n_exp, block_rows)).astype(jnp.bfloat16))
    listed_slot = jnp.where(listed_rank < late, early + listed_rank, over_first + listed_rank - late)
    plain_slot = jnp.where((plain_rank < over_first) | (over < 0.5), plain_rank, plain_rank + over)
    plain_slot = jnp.where(plain_slot < early, plain_slot, plain_rank + jnp.minimum(listed_count, late))
    slot_of = jnp.sum(named_listed * listed_slot + named_plain * plain_slot, axis=0, keepdims=True).astype(jnp.int32)

    def seats(size, count, kept):
        key = jnp.where(kept, expert * count + slot_of - size, -1)
        return one_hot(key == lax.broadcasted_iota(jnp.int32, (n_exp * count, block_rows), 0))

    seat = seats(0, capacity, slot_of >= 0)
    late_seat = seats(early, late, slot_of >= early) if early else seat
    gain = gain_ref[...].astype(jnp.float32).reshape(1, width)
    if early:
        plain = (unit_rms(tokens_ref[...].astype(jnp.float32)) * gain).astype(jnp.bfloat16)
        early_seat = seats(0, early, (slot_of < early) & jnp.logical_not(is_listed))
        outbound_early[...] = dot(early_seat, plain).astype(jnp.bfloat16).reshape(n_exp, early, width)
        over_seat = (slot_of == lax.broadcasted_iota(jnp.int32, (early, block_rows), 0)) & is_listed
        over_name = jnp.sum(jnp.where(over_seat, (expert + 1).astype(jnp.float32), 0.0), axis=1, keepdims=True)

    pl.semaphore_wait(barrier, n_head - 1 + n_qp - 1)
    for k in range(1, n_qp):
        pl.semaphore_signal(entered, inc=1, device_id={"qp": (qp + k) % n_qp}, device_id_type=MESH)

    sends = []

    def start(copy):
        copy.start()
        sends.append(copy)

    for k in range(1, n_head):
        to = flip(my_head, n_head - k)
        start(remote(pick.at[to], head.at[my_head], a_send.at[k], a_recv.at[k], head_device(to)))
        if tail:
            start(remote(pick_tail.at[to], head_tail.at[my_head], a_send.at[n_head + k], a_recv.at[n_head + k], head_device(to)))
    a_sends = sends[:]
    sends.clear()
    for k in range(1, n_rep):
        to = {"rep": (rep + k) % n_rep}
        for at, (src, dst) in enumerate(((gate_any, gate_w), (up_any, up_w), (down_any, down_w))):
            start(remote(src.at[0], dst.at[rep], w_send.at[k, at], w_recv.at[k, at], to))
    head[my_head] = pick[my_head]
    if tail:
        head_tail[my_head] = pick_tail[my_head]

    for copy in a_sends:
        copy.wait_send()
    if n_qp > 1:
        pl.semaphore_wait(entered, n_qp - 1)
    if early:
        for k in [0, 4, 5, 6]:
            to = flip(my_exp, n_exp - 1 - k)
            start(remote(outbound_early.at[to], arrived.at[k, pl.ds(0, early)], f_send.at[k], f_recv.at[k], exp_device(to)))
    local[0].wait()
    local[1].wait()
    for k in range(1, n_head):
        source = flip(my_head, n_head - k)
        remote(pick.at[source], head.at[source], a_send.at[k], a_recv.at[k], head_device(source)).wait_recv()
        if tail:
            remote(pick_tail.at[source], head_tail.at[source], a_send.at[n_head + k], a_recv.at[n_head + k], head_device(source)).wait_recv()

    if early:
        for k in [1, 2, 3]:
            to = flip(my_exp, n_exp - 1 - k)
            start(remote(outbound_early.at[to], arrived.at[k, pl.ds(0, early)], f_send.at[k], f_recv.at[k], exp_device(to)))
        arrived[n_exp - 1, :early] = outbound_early[my_exp]
    head_rows = join_rows(head, head_tail, 0, width).astype(jnp.bfloat16)
    projected = dot(head_rows, qkv[...])
    queries = unit_rms(projected[:, :head_width]).astype(jnp.bfloat16)
    keyval[qp, :, :head_width] = unit_rms(projected[:, head_width : 2 * head_width]).astype(jnp.bfloat16)
    keyval[qp, :, head_width : 2 * head_width] = projected[:, 2 * head_width :].astype(jnp.bfloat16)
    table = jnp.max(borne[:, :, width : width + slot_count].astype(jnp.float32), axis=1)
    keyval[qp, :, 2 * head_width :] = jnp.broadcast_to(places(table.astype(jnp.bfloat16)), (rows, LANES)).astype(jnp.bfloat16)
    for k in range(1, n_qp):
        start(remote(keyval.at[qp], keyval.at[qp], b_send.at[k], b_recv.at[k], {"qp": (qp + k) % n_qp}))

    base_block = block_of + steps(block_of, n_rep, n_tok) * ((n_qp - 1) * n_rep)

    def positions(source):
        inside = keyval[source, :, 2 * head_width :].astype(jnp.float32)
        base = ((base_block + source * n_rep) * block_rows).astype(jnp.float32)
        return jnp.where(inside >= 0.0, base + inside, all_tokens)

    query_places = positions(qp)[:, :1]
    head_gate = jax.nn.sigmoid(
        jnp.sum(head_rows.astype(jnp.float32) * select_ref[...].astype(jnp.float32), axis=1, keepdims=True)
    )
    head_gate = jnp.where(query_places < all_tokens, head_gate, 0.0)
    numerator = jnp.zeros((rows, head_width), jnp.float32)
    denominator = jnp.zeros((rows, 1), jnp.float32)
    for k in range(n_qp):
        source = (qp + n_qp - k) % n_qp
        if k:
            remote(keyval.at[source], keyval.at[source], b_send.at[k], b_recv.at[k], {"qp": source}).wait_recv()
        key_places = jnp.transpose(positions(source))[:1]
        scores = dot(queries, keyval[source, :, :head_width], ((1,), (1,))) * head_width**-0.5
        weights = jnp.where(key_places <= query_places, jnp.exp(scores), 0.0)
        denominator = denominator + jnp.sum(weights, axis=1, keepdims=True)
        numerator = numerator + dot(
            weights.astype(jnp.bfloat16), keyval[source, :, head_width : 2 * head_width]
        )
    attended = (numerator / denominator).astype(jnp.bfloat16)
    split_rows(dot(attended, wout[...]) * head_gate, contrib, contrib_tail, 0, width)
    for k in range(1, n_head):
        to = flip(my_head, n_head - k)
        start(remote(contrib.at[to], returned.at[my_head], c_send.at[k], c_recv.at[k], head_device(to)))
        if tail:
            start(remote(contrib_tail.at[to], returned_tail.at[my_head], c_send.at[n_head + k], c_recv.at[n_head + k], head_device(to)))
    returned[my_head] = contrib[my_head]
    if tail:
        returned_tail[my_head] = contrib_tail[my_head]
    for k in range(1, n_head):
        source = flip(my_head, n_head - k)
        remote(contrib.at[source], returned.at[source], c_send.at[k], c_recv.at[k], head_device(source)).wait_recv()
        if tail:
            remote(contrib_tail.at[source], returned_tail.at[source], c_send.at[n_head + k], c_recv.at[n_head + k], head_device(source)).wait_recv()

    attention = dot(chosen, join_rows(returned, returned_tail, 0, width).astype(jnp.bfloat16), ((0,), (0,)))
    residual = tokens_ref[...].astype(jnp.float32) + attention
    residual_ref[...] = residual
    normed = (unit_rms(residual) * gain).astype(jnp.bfloat16)
    half = n_exp // 2
    partner = flip(my_exp, half)
    if early:
        over_out[:, :width] = dot(one_hot(over_seat), normed).astype(jnp.bfloat16)
        over_out[:, width:] = jnp.broadcast_to(over_name, (early, LANES)).astype(jnp.bfloat16)
        for m in [half, *range(1, half)]:
            to = flip(my_exp, m)
            start(remote(over_out, over_in.at[my_exp], o_send.at[m], o_recv.at[m], exp_device(to)))
        over_in[my_exp] = over_out[...]
    outbound[...] = dot(late_seat, normed).astype(jnp.bfloat16).reshape(n_exp, late, width)

    def late_part(k):
        return arrived.at[k, pl.ds(early, late)]

    for k in range(n_exp - 1):
        to = flip(my_exp, n_exp - 1 - k)
        start(remote(outbound.at[to], late_part(k), d_send.at[k], d_recv.at[k], exp_device(to)))
    arrived[n_exp - 1, early:] = outbound[my_exp]
    if early:
        remote(over_out, over_in.at[partner], o_send.at[half], o_recv.at[half], exp_device(partner)).wait_recv()
        for m in range(1, half):
            to = flip(my_exp, m)
            start(remote(over_in.at[partner], over_in.at[partner], o_send.at[half + m], o_recv.at[half + m], exp_device(to)))

    for copy in local[2:]:
        copy.wait()
    for k in range(1, n_rep):
        source = (rep + n_rep - k) % n_rep
        for at, (src, dst) in enumerate(((gate_any, gate_w), (up_any, up_w), (down_any, down_w))):
            remote(src.at[0], dst.at[source], w_send.at[k, at], w_recv.at[k, at], {"rep": source}).wait_recv()

    if early:
        for m in range(1, half):
            beside = flip(my_exp, m)
            beyond = flip(beside, half)
            remote(over_out, over_in.at[beside], o_send.at[m], o_recv.at[m], exp_device(beside)).wait_recv()
            remote(over_in.at[beyond], over_in.at[beyond], o_send.at[half + m], o_recv.at[half + m], exp_device(beside)).wait_recv()

    group = n_exp // groups
    for first in range(0, n_exp, group):
        for k in range(first, min(first + group, n_exp - 1)):
            source = flip(my_exp, n_exp - 1 - k)
            if early:
                remote(outbound_early.at[source], arrived.at[k, pl.ds(0, early)], f_send.at[k], f_recv.at[k], exp_device(source)).wait_recv()
            remote(outbound.at[source], late_part(k), d_send.at[k], d_recv.at[k], exp_device(source)).wait_recv()
        for k in range(first, first + group if early else first):
            block = flip(my_exp, n_exp - 1 - k)
            extra = over_in[block].astype(jnp.float32)
            here = arrived[k, :early].astype(jnp.float32)
            taken = extra[:, width : width + 1] == (my_exp + 1).astype(jnp.float32)
            arrived[k, :early] = jnp.where(taken, extra[:, :width], here).astype(jnp.bfloat16)
        flat = arrived[first : first + group].reshape(group * capacity, width)
        total = jnp.zeros((group * capacity, width), jnp.float32)
        for part in range(n_rep):
            hidden = (jax.nn.silu(dot(flat, gate_w[part])) * dot(flat, up_w[part])).astype(jnp.bfloat16)
            total = total + dot(hidden, down_w[part])
        router_gate = jax.nn.sigmoid(
            jnp.sum(flat.astype(jnp.float32) * router_ref[...].astype(jnp.float32), axis=1, keepdims=True)
        )
        leaving[first : first + group] = (total * router_gate).astype(jnp.bfloat16).reshape(group, capacity, width)
        for k in range(first, min(first + group, n_exp - 1)):
            source = flip(my_exp, n_exp - 1 - k)
            start(remote(leaving.at[k], back.at[my_exp], e_send.at[k], e_recv.at[k], exp_device(source)))
    back[my_exp] = leaving[n_exp - 1]
    for k in range(n_exp - 1):
        owner = flip(my_exp, n_exp - 1 - k)
        remote(leaving.at[k], back.at[owner], e_send.at[k], e_recv.at[k], exp_device(owner)).wait_recv()
    routed = dot(seat, back[...].reshape(n_exp * capacity, width), ((0,), (0,)))
    out_ref[...] = (residual_ref[...] + routed).astype(out_ref.dtype)
    for copy in sends:
        copy.wait_send()


def local(
    mesh_sizes, tokens, listed, w_qkv, w_out, w_select, norm_gain, expert_id, router, w_gate, w_up, w_down
):
    n_tok, n_qp, n_rep = mesh_sizes
    n_head, n_exp = n_tok * n_rep, n_tok * n_qp
    block_rows, width = tokens.shape
    assert n_head & (n_head - 1) == 0 and n_exp & (n_exp - 1) == 0
    slot_count = listed.shape[2]
    head_width = w_out.shape[1]
    assert listed.shape[1] == n_head and w_out.shape[0] == 1 and w_gate.shape[0] == 1
    assert block_rows <= 2 * LANES
    main = slot_count // 8 * 8
    tail = 1 << (slot_count - main - 1).bit_length() if slot_count > main else 0
    assert main
    slots = main + tail
    capacity = round_up(max(2, 2 * block_rows // n_exp), ROW_TILE)
    listed_most = n_head * slot_count
    kept = capacity - ROW_TILE
    most_over = max(min(listed_most, capacity * k) - kept * k for k in range(1, n_exp + 1))
    early = ROW_TILE if n_exp > 1 and kept >= ROW_TILE and most_over <= ROW_TILE else 0
    groups = min(n_exp, 8)
    rows = n_head * slots
    bf16 = jnp.bfloat16
    dma = pltpu.SemaphoreType.DMA
    vmem, anywhere = pl.BlockSpec(memory_space=pltpu.VMEM), pl.BlockSpec(memory_space=pltpu.HBM)
    hidden = w_gate.shape[2]
    tail_count = n_head if tail else 0
    small = [tokens, listed, expert_id.reshape(1, -1), norm_gain, w_select, router]
    scratch = [pltpu.VMEM(array.shape, array.dtype) for array in small]
    scratch += [
        pltpu.VMEM((n_head, main, width if tail else width + LANES), bf16),
        pltpu.VMEM((n_head, main, width if tail else width + LANES), bf16),
        pltpu.VMEM((n_qp, rows, 2 * head_width + LANES), bf16),
        pltpu.VMEM((n_head, main, width), bf16),
        pltpu.VMEM((n_head, main, width), bf16),
        pltpu.VMEM((tail_count, tail, width + LANES), bf16),
        pltpu.VMEM((tail_count, tail, width + LANES), bf16),
        pltpu.VMEM((tail_count, tail, width), bf16),
        pltpu.VMEM((tail_count, tail, width), bf16),
        pltpu.VMEM((block_rows, width), jnp.float32),
        pltpu.VMEM((n_exp, capacity - early, width), bf16),
        pltpu.VMEM((n_exp if early else 1, ROW_TILE, width), bf16),
        pltpu.VMEM((ROW_TILE, width + LANES), bf16),
        pltpu.VMEM((n_exp if early else 1, ROW_TILE, width + LANES), bf16),
        pltpu.VMEM((n_exp, capacity, width), bf16),
        pltpu.VMEM((n_exp, capacity, width), bf16),
        pltpu.VMEM((n_exp, capacity, width), bf16),
        pltpu.VMEM(w_qkv.shape[1:], bf16),
        pltpu.VMEM(w_out.shape[1:], bf16),
        pltpu.VMEM((n_rep, width, hidden), bf16),
        pltpu.VMEM((n_rep, width, hidden), bf16),
        pltpu.VMEM((n_rep, hidden, width), bf16),
    ]
    semaphores = [(len(small),), (5,), (2 * n_head,), (2 * n_head,), (n_rep, 3), (n_rep, 3), (n_qp,), (n_qp,)]
    semaphores += [(2 * n_head,), (2 * n_head,), *[(n_exp,)] * 8]
    return pl.pallas_call(
        functools.partial(layer_kernel, (n_tok, n_qp, n_rep, main, tail, capacity, early, groups)),
        out_shape=pltpu.VMEM((block_rows, width), bf16),
        in_specs=[anywhere] * 11,
        out_specs=vmem,
        scratch_shapes=scratch + [pltpu.SemaphoreType.REGULAR] + [dma(shape) for shape in semaphores],
        compiler_params=pltpu.CompilerParams(
            collective_id=0, has_side_effects=True, vmem_limit_bytes=60 << 20
        ),
    )(
        *small,
        w_qkv,
        w_out,
        w_gate,
        w_up,
        w_down,
    )


def solution(mesh):
    in_specs = (
        P(("group", "tok", "qp", "rep"), None),
        P(("group", "tok", "qp", "rep"), None, None),
        P(("tok", "rep"), None, None),
        P(("tok", "rep"), None, None),
        P(("tok", "rep"), None),
        P(),
        P(("group", "tok", "qp", "rep"), None),
        P(("tok", "qp"), None),
        P(("tok", "qp"), None, "rep"),
        P(("tok", "qp"), None, "rep"),
        P(("tok", "qp"), "rep", None),
    )
    out_specs = P(("group", "tok", "qp", "rep"), None)
    sizes = (mesh.shape["tok"], mesh.shape["qp"], mesh.shape["rep"])
    return jax.shard_map(
        functools.partial(local, sizes), mesh=mesh, in_specs=in_specs, out_specs=out_specs, check_vma=False
    )
```

```python
import functools
import jax
import jax.numpy as jnp
from jax import lax
from jax.experimental import pallas as pl
from jax.experimental.pallas import tpu as pltpu
from jax.sharding import PartitionSpec as P

MESH = pl.DeviceIdType.MESH
LANES = 128
ROW_TILE = 16


def round_up(value, step):
    return -(-value // step) * step


def unit_rms(values):
    return values * lax.rsqrt(jnp.mean(values * values, axis=-1, keepdims=True) + 1e-06)


def dot(left, right, dims=((1,), (0,))):
    return lax.dot_general(left, right, (dims, ((), ())), preferred_element_type=jnp.float32)


def steps(index, size, count):
    return sum(((index >= m * size).astype(jnp.int32) for m in range(1, count)), jnp.zeros_like(index))


def split_rows(values, main_ref, tail_ref, first, last):
    count, main, _ = main_ref.shape
    main_ref[:, :, first:last] = values[: count * main].reshape(count, main, last - first).astype(main_ref.dtype)
    if tail_ref.shape[0]:
        tail = tail_ref.shape[1]
        for at in range(count):
            here = count * main + at * tail
            tail_ref[at, :, first:last] = values[here : here + tail].astype(tail_ref.dtype)


def join_rows(main_ref, tail_ref, first, last):
    count, main, _ = main_ref.shape
    parts = [main_ref[:, :, first:last].astype(jnp.float32).reshape(count * main, last - first)]
    parts += [tail_ref[at, :, first:last].astype(jnp.float32) for at in range(tail_ref.shape[0])]
    return jnp.concatenate(parts, axis=0)


def flip(index, mask):
    moved, bit = index, 1
    while bit <= mask:
        if mask & bit:
            moved = moved + bit * (1 - 2 * ((index // bit) % 2))
        bit *= 2
    return moved


def one_hot(mask):
    return jnp.where(mask, 1.0, 0.0).astype(jnp.bfloat16)


def layer_kernel(
    sizes,
    tokens_any,
    listed_any,
    expert_any,
    gain_any,
    select_any,
    router_any,
    qkv_any,
    wout_any,
    gate_any,
    up_any,
    down_any,
    out_ref,
    tokens_ref,
    listed_ref,
    expert_ref,
    gain_ref,
    select_ref,
    router_ref,
    pick,
    head,
    keyval,
    contrib,
    returned,
    pick_tail,
    head_tail,
    contrib_tail,
    returned_tail,
    residual_ref,
    late_seat_ref,
    outbound,
    outbound_early,
    over_out,
    over_in,
    arrived,
    leaving,
    back,
    qkv,
    wout,
    gate_w,
    up_w,
    down_w,
    entered,
    small_sem,
    local_sem,
    a_send,
    a_recv,
    w_send,
    w_recv,
    b_send,
    b_recv,
    c_send,
    c_recv,
    d_send,
    d_recv,
    f_send,
    f_recv,
    o_send,
    o_recv,
    e_send,
    e_recv,
):
    n_tok, n_qp, n_rep, main, tail, capacity, early, groups = sizes
    n_head, n_exp = n_tok * n_rep, n_tok * n_qp
    block_rows, width = tokens_ref.shape
    head_width = wout.shape[0]
    main_rows, rows = n_head * main, n_head * (main + tail)
    all_tokens = float(n_exp * n_rep * block_rows)
    tok, qp, rep = lax.axis_index("tok"), lax.axis_index("qp"), lax.axis_index("rep")
    my_head = tok * n_rep + rep
    my_exp = tok * n_qp + qp

    def head_device(index):
        return {"tok": index // n_rep, "rep": index % n_rep}

    def exp_device(index):
        return {"tok": index // n_qp, "qp": index % n_qp}

    def remote(src, dst, send, recv, device):
        return pltpu.make_async_remote_copy(
            src_ref=src, dst_ref=dst, send_sem=send, recv_sem=recv, device_id=device, device_id_type=MESH
        )

    barrier = pltpu.get_barrier_semaphore()
    for k in range(1, n_head):
        pl.semaphore_signal(barrier, inc=1, device_id=head_device((my_head + k) % n_head), device_id_type=MESH)
    for k in range(1, n_qp):
        pl.semaphore_signal(barrier, inc=1, device_id={"qp": (qp + k) % n_qp}, device_id_type=MESH)

    small = [
        pltpu.make_async_copy(src, dst, small_sem.at[at])
        for at, (src, dst) in enumerate(
            (
                (listed_any, listed_ref),
                (tokens_any, tokens_ref),
                (expert_any, expert_ref),
                (gain_any, gain_ref),
                (select_any, select_ref),
                (router_any, router_ref),
            )
        )
    ]
    for copy in small:
        copy.start()
    local = [
        pltpu.make_async_copy(qkv_any.at[0], qkv, local_sem.at[0]),
        pltpu.make_async_copy(wout_any.at[0], wout, local_sem.at[1]),
        pltpu.make_async_copy(gate_any.at[0], gate_w.at[rep], local_sem.at[2]),
        pltpu.make_async_copy(up_any.at[0], up_w.at[rep], local_sem.at[3]),
        pltpu.make_async_copy(down_any.at[0], down_w.at[rep], local_sem.at[4]),
    ]
    for copy in local:
        copy.start()

    row_index = lax.broadcasted_iota(jnp.int32, (rows, 1), 0)
    block_of = steps(row_index, main, n_head)
    within = row_index - block_of * main
    if tail:
        tail_index = row_index - main_rows
        tail_block = steps(tail_index, tail, n_head)
        block_of = jnp.where(tail_index >= 0, tail_block, block_of)
        within = jnp.where(tail_index >= 0, main + tail_index - tail_block * tail, within)
    slot_count = listed_ref.shape[2]
    small[0].wait()
    spread = one_hot(block_of == lax.broadcasted_iota(jnp.int32, (rows, n_head), 1))
    at_slot = within == lax.broadcasted_iota(jnp.int32, (rows, slot_count), 1)

    def places(table):
        of_row = jnp.sum(jnp.where(at_slot, dot(spread, table), 0.0), axis=1, keepdims=True)
        return jnp.where(within < slot_count, of_row, -1.0)

    table = listed_ref[0].astype(jnp.float32)
    place = places(table.astype(jnp.bfloat16))
    lane_index = lax.broadcasted_iota(jnp.int32, (rows, block_rows), 1)
    chosen = one_hot(place.astype(jnp.int32) == lane_index)
    small[1].wait()
    picked = dot(chosen, tokens_ref[...])
    split_rows(picked, pick, pick_tail, 0, width)
    bearer, borne = (pick_tail, head_tail) if tail else (pick, head)
    bearer[:, :, width : width + slot_count] = jnp.broadcast_to(
        table[:, None, :], (n_head, bearer.shape[1], slot_count)
    ).astype(jnp.bfloat16)

    for copy in small[2:]:
        copy.wait()
    expert = expert_ref[...]
    late = capacity - early
    is_listed = jnp.sum(chosen.astype(jnp.float32), axis=0, keepdims=True) > 0.0
    named = expert == lax.broadcasted_iota(jnp.int32, (n_exp, block_rows), 0)
    named_listed = jnp.where(named & is_listed, 1.0, 0.0)
    named_plain = jnp.where(named, 1.0, 0.0) - named_listed
    earlier = one_hot(
        lax.broadcasted_iota(jnp.int32, (block_rows, block_rows), 0)
        <= lax.broadcasted_iota(jnp.int32, (block_rows, block_rows), 1)
    )
    listed_rank = dot(named_listed.astype(jnp.bfloat16), earlier) - 1.0
    plain_rank = dot(named_plain.astype(jnp.bfloat16), earlier) - 1.0
    listed_count = jnp.sum(named_listed, axis=1, keepdims=True)
    over = jnp.maximum(listed_count - late, 0.0)
    below = one_hot(
        lax.broadcasted_iota(jnp.int32, (n_exp, n_exp), 1) < lax.broadcasted_iota(jnp.int32, (n_exp, n_exp), 0)
    )
    over_first = dot(below, jnp.broadcast_to(over, (n_exp, block_rows)).astype(jnp.bfloat16))
    listed_slot = jnp.where(listed_rank < late, early + listed_rank, over_first + listed_rank - late)
    plain_slot = jnp.where((plain_rank < over_first) | (over < 0.5), plain_rank, plain_rank + over)
    plain_slot = jnp.where(plain_slot < early, plain_slot, plain_rank + jnp.minimum(listed_count, late))
    slot_of = jnp.sum(named_listed * listed_slot + named_plain * plain_slot, axis=0, keepdims=True).astype(jnp.int32)

    def seats(size, count, kept):
        key = jnp.where(kept, expert * count + slot_of - size, -1)
        return one_hot(key == lax.broadcasted_iota(jnp.int32, (n_exp * count, block_rows), 0))

    seat = seats(0, capacity, slot_of >= 0)
    late_seat = seats(early, late, slot_of >= early) if early else seat
    late_seat_ref[...] = late_seat
    gain = gain_ref[...].astype(jnp.float32).reshape(1, width)
    if early:
        plain = (unit_rms(tokens_ref[...].astype(jnp.float32)) * gain).astype(jnp.bfloat16)
        early_seat = seats(0, early, (slot_of < early) & jnp.logical_not(is_listed))
        outbound_early[...] = dot(early_seat, plain).astype(jnp.bfloat16).reshape(n_exp, early, width)
        over_seat = (slot_of == lax.broadcasted_iota(jnp.int32, (early, block_rows), 0)) & is_listed
        over_name = jnp.sum(jnp.where(over_seat, (expert + 1).astype(jnp.float32), 0.0), axis=1, keepdims=True)

    pl.semaphore_wait(barrier, n_head - 1 + n_qp - 1)
    for k in range(1, n_qp):
        pl.semaphore_signal(entered, inc=1, device_id={"qp": (qp + k) % n_qp}, device_id_type=MESH)

    sends = []

    def start(copy):
        copy.start()
        sends.append(copy)

    for k in range(1, n_head):
        to = flip(my_head, n_head - k)
        start(remote(pick.at[to], head.at[my_head], a_send.at[k], a_recv.at[k], head_device(to)))
        if tail:
            start(remote(pick_tail.at[to], head_tail.at[my_head], a_send.at[n_head + k], a_recv.at[n_head + k], head_device(to)))
    a_sends = sends[:]
    sends.clear()
    head[my_head] = pick[my_head]
    if tail:
        head_tail[my_head] = pick_tail[my_head]

    for copy in a_sends:
        copy.wait_send()
    if n_qp > 1:
        pl.semaphore_wait(entered, n_qp - 1)
    if early:
        for k in [0, 4, 5, 6]:
            to = flip(my_exp, n_exp - 1 - k)
            start(remote(outbound_early.at[to], arrived.at[k, pl.ds(0, early)], f_send.at[k], f_recv.at[k], exp_device(to)))
    local[0].wait()
    local[1].wait()
    for k in range(1, n_head):
        source = flip(my_head, n_head - k)
        remote(pick.at[source], head.at[source], a_send.at[k], a_recv.at[k], head_device(source)).wait_recv()
        if tail:
            remote(pick_tail.at[source], head_tail.at[source], a_send.at[n_head + k], a_recv.at[n_head + k], head_device(source)).wait_recv()

    if early:
        for k in [1, 2, 3]:
            to = flip(my_exp, n_exp - 1 - k)
            start(remote(outbound_early.at[to], arrived.at[k, pl.ds(0, early)], f_send.at[k], f_recv.at[k], exp_device(to)))
        arrived[n_exp - 1, :early] = outbound_early[my_exp]
    head_rows = join_rows(head, head_tail, 0, width).astype(jnp.bfloat16)
    projected = dot(head_rows, qkv[...])
    queries = unit_rms(projected[:, :head_width]).astype(jnp.bfloat16)
    keyval[qp, :, :head_width] = unit_rms(projected[:, head_width : 2 * head_width]).astype(jnp.bfloat16)
    keyval[qp, :, head_width : 2 * head_width] = projected[:, 2 * head_width :].astype(jnp.bfloat16)
    table = jnp.max(borne[:, :, width : width + slot_count].astype(jnp.float32), axis=1)
    keyval[qp, :, 2 * head_width :] = jnp.broadcast_to(places(table.astype(jnp.bfloat16)), (rows, LANES)).astype(jnp.bfloat16)
    for k in range(1, n_qp):
        start(remote(keyval.at[qp], keyval.at[qp], b_send.at[k], b_recv.at[k], {"qp": (qp + k) % n_qp}))

    base_block = block_of + steps(block_of, n_rep, n_tok) * ((n_qp - 1) * n_rep)

    def positions(source):
        inside = keyval[source, :, 2 * head_width :].astype(jnp.float32)
        base = ((base_block + source * n_rep) * block_rows).astype(jnp.float32)
        return jnp.where(inside >= 0.0, base + inside, all_tokens)

    query_places = positions(qp)[:, :1]
    head_gate = jax.nn.sigmoid(
        jnp.sum(head_rows.astype(jnp.float32) * select_ref[...].astype(jnp.float32), axis=1, keepdims=True)
    )
    head_gate = jnp.where(query_places < all_tokens, head_gate, 0.0)
    numerator = jnp.zeros((rows, head_width), jnp.float32)
    denominator = jnp.zeros((rows, 1), jnp.float32)
    for k in range(n_qp):
        source = (qp + n_qp - k) % n_qp
        if k:
            remote(keyval.at[source], keyval.at[source], b_send.at[k], b_recv.at[k], {"qp": source}).wait_recv()
        key_places = jnp.transpose(positions(source))[:1]
        scores = dot(queries, keyval[source, :, :head_width], ((1,), (1,))) * head_width**-0.5
        weights = jnp.where(key_places <= query_places, jnp.exp(scores), 0.0)
        denominator = denominator + jnp.sum(weights, axis=1, keepdims=True)
        numerator = numerator + dot(
            weights.astype(jnp.bfloat16), keyval[source, :, head_width : 2 * head_width]
        )
    attended = (numerator / denominator).astype(jnp.bfloat16)
    split_rows(dot(attended, wout[...]) * head_gate, contrib, contrib_tail, 0, width)
    for k in range(1, n_head):
        to = flip(my_head, n_head - k)
        start(remote(contrib.at[to], returned.at[my_head], c_send.at[k], c_recv.at[k], head_device(to)))
        if tail:
            start(remote(contrib_tail.at[to], returned_tail.at[my_head], c_send.at[n_head + k], c_recv.at[n_head + k], head_device(to)))
    for k in range(1, n_rep):
        to = {"rep": (rep + k) % n_rep}
        for at, (src, dst) in enumerate(((gate_any, gate_w), (up_any, up_w), (down_any, down_w))):
            start(remote(src.at[0], dst.at[rep], w_send.at[k, at], w_recv.at[k, at], to))
    returned[my_head] = contrib[my_head]
    if tail:
        returned_tail[my_head] = contrib_tail[my_head]
    for k in range(1, n_head):
        source = flip(my_head, n_head - k)
        remote(contrib.at[source], returned.at[source], c_send.at[k], c_recv.at[k], head_device(source)).wait_recv()
        if tail:
            remote(contrib_tail.at[source], returned_tail.at[source], c_send.at[n_head + k], c_recv.at[n_head + k], head_device(source)).wait_recv()

    attention = dot(chosen, join_rows(returned, returned_tail, 0, width).astype(jnp.bfloat16), ((0,), (0,)))
    residual = tokens_ref[...].astype(jnp.float32) + attention
    residual_ref[...] = residual
    normed = (unit_rms(residual) * gain).astype(jnp.bfloat16)
    half = n_exp // 2
    partner = flip(my_exp, half)
    if early:
        over_out[:, :width] = dot(one_hot(over_seat), normed).astype(jnp.bfloat16)
        over_out[:, width:] = jnp.broadcast_to(over_name, (early, LANES)).astype(jnp.bfloat16)
        for m in [half, *range(1, half)]:
            to = flip(my_exp, m)
            start(remote(over_out, over_in.at[my_exp], o_send.at[m], o_recv.at[m], exp_device(to)))
        over_in[my_exp] = over_out[...]
    def late_part(k):
        return arrived.at[k, pl.ds(early, late)]

    def send_late(k):
        to = flip(my_exp, n_exp - 1 - k)
        start(remote(outbound.at[to], late_part(k), d_send.at[k], d_recv.at[k], exp_device(to)))

    far_first = (1 - my_exp // half) * half
    near_first = half - far_first
    for first in (far_first, near_first):
        part = late_seat_ref[pl.ds(first * late, half * late), :]
        outbound[pl.ds(first, half)] = dot(part, normed).astype(jnp.bfloat16).reshape(half, late, width)
        if first is far_first:
            for k in range(half):
                send_late(k)

    for k in range(half, n_exp - 1):
        send_late(k)
    arrived[n_exp - 1, early:] = outbound[my_exp]
    if early:
        remote(over_out, over_in.at[partner], o_send.at[half], o_recv.at[half], exp_device(partner)).wait_recv()
        for m in range(1, half):
            to = flip(my_exp, m)
            start(remote(over_in.at[partner], over_in.at[partner], o_send.at[half + m], o_recv.at[half + m], exp_device(to)))

    for copy in local[2:]:
        copy.wait()
    for k in range(1, n_rep):
        source = (rep + n_rep - k) % n_rep
        for at, (src, dst) in enumerate(((gate_any, gate_w), (up_any, up_w), (down_any, down_w))):
            remote(src.at[0], dst.at[source], w_send.at[k, at], w_recv.at[k, at], {"rep": source}).wait_recv()

    if early:
        for m in range(1, half):
            beside = flip(my_exp, m)
            beyond = flip(beside, half)
            remote(over_out, over_in.at[beside], o_send.at[m], o_recv.at[m], exp_device(beside)).wait_recv()
            remote(over_in.at[beyond], over_in.at[beyond], o_send.at[half + m], o_recv.at[half + m], exp_device(beside)).wait_recv()

    group = n_exp // groups
    for first in range(0, n_exp, group):
        for k in range(first, min(first + group, n_exp - 1)):
            source = flip(my_exp, n_exp - 1 - k)
            if early:
                remote(outbound_early.at[source], arrived.at[k, pl.ds(0, early)], f_send.at[k], f_recv.at[k], exp_device(source)).wait_recv()
            remote(outbound.at[source], late_part(k), d_send.at[k], d_recv.at[k], exp_device(source)).wait_recv()
        for k in range(first, first + group if early else first):
            block = flip(my_exp, n_exp - 1 - k)
            extra = over_in[block].astype(jnp.float32)
            here = arrived[k, :early].astype(jnp.float32)
            taken = extra[:, width : width + 1] == (my_exp + 1).astype(jnp.float32)
            arrived[k, :early] = jnp.where(taken, extra[:, :width], here).astype(jnp.bfloat16)
        flat = arrived[first : first + group].reshape(group * capacity, width)
        total = jnp.zeros((group * capacity, width), jnp.float32)
        for part in range(n_rep):
            hidden = (jax.nn.silu(dot(flat, gate_w[part])) * dot(flat, up_w[part])).astype(jnp.bfloat16)
            total = total + dot(hidden, down_w[part])
        router_gate = jax.nn.sigmoid(
            jnp.sum(flat.astype(jnp.float32) * router_ref[...].astype(jnp.float32), axis=1, keepdims=True)
        )
        leaving[first : first + group] = (total * router_gate).astype(jnp.bfloat16).reshape(group, capacity, width)
        for k in range(first, min(first + group, n_exp - 1)):
            source = flip(my_exp, n_exp - 1 - k)
            start(remote(leaving.at[k], back.at[my_exp], e_send.at[k], e_recv.at[k], exp_device(source)))
    back[my_exp] = leaving[n_exp - 1]
    for k in range(n_exp - 1):
        owner = flip(my_exp, n_exp - 1 - k)
        remote(leaving.at[k], back.at[owner], e_send.at[k], e_recv.at[k], exp_device(owner)).wait_recv()
    routed = dot(seat, back[...].reshape(n_exp * capacity, width), ((0,), (0,)))
    out_ref[...] = (residual_ref[...] + routed).astype(out_ref.dtype)
    for copy in sends:
        copy.wait_send()


def local(
    mesh_sizes, tokens, listed, w_qkv, w_out, w_select, norm_gain, expert_id, router, w_gate, w_up, w_down
):
    n_tok, n_qp, n_rep = mesh_sizes
    n_head, n_exp = n_tok * n_rep, n_tok * n_qp
    block_rows, width = tokens.shape
    assert n_head & (n_head - 1) == 0 and n_exp & (n_exp - 1) == 0
    slot_count = listed.shape[2]
    head_width = w_out.shape[1]
    assert listed.shape[1] == n_head and w_out.shape[0] == 1 and w_gate.shape[0] == 1
    assert block_rows <= 2 * LANES
    main = slot_count // 8 * 8
    tail = 1 << (slot_count - main - 1).bit_length() if slot_count > main else 0
    assert main
    slots = main + tail
    capacity = round_up(max(2, 2 * block_rows // n_exp), ROW_TILE)
    listed_most = n_head * slot_count
    kept = capacity - ROW_TILE
    most_over = max(min(listed_most, capacity * k) - kept * k for k in range(1, n_exp + 1))
    early = ROW_TILE if n_exp > 1 and kept >= ROW_TILE and most_over <= ROW_TILE else 0
    groups = min(n_exp, 8)
    rows = n_head * slots
    bf16 = jnp.bfloat16
    dma = pltpu.SemaphoreType.DMA
    vmem, anywhere = pl.BlockSpec(memory_space=pltpu.VMEM), pl.BlockSpec(memory_space=pltpu.HBM)
    hidden = w_gate.shape[2]
    tail_count = n_head if tail else 0
    small = [tokens, listed, expert_id.reshape(1, -1), norm_gain, w_select, router]
    scratch = [pltpu.VMEM(array.shape, array.dtype) for array in small]
    scratch += [
        pltpu.VMEM((n_head, main, width if tail else width + LANES), bf16),
        pltpu.VMEM((n_head, main, width if tail else width + LANES), bf16),
        pltpu.VMEM((n_qp, rows, 2 * head_width + LANES), bf16),
        pltpu.VMEM((n_head, main, width), bf16),
        pltpu.VMEM((n_head, main, width), bf16),
        pltpu.VMEM((tail_count, tail, width + LANES), bf16),
        pltpu.VMEM((tail_count, tail, width + LANES), bf16),
        pltpu.VMEM((tail_count, tail, width), bf16),
        pltpu.VMEM((tail_count, tail, width), bf16),
        pltpu.VMEM((block_rows, width), jnp.float32),
        pltpu.VMEM((n_exp * (capacity - early), block_rows), bf16),
        pltpu.VMEM((n_exp, capacity - early, width), bf16),
        pltpu.VMEM((n_exp if early else 1, ROW_TILE, width), bf16),
        pltpu.VMEM((ROW_TILE, width + LANES), bf16),
        pltpu.VMEM((n_exp if early else 1, ROW_TILE, width + LANES), bf16),
        pltpu.VMEM((n_exp, capacity, width), bf16),
        pltpu.VMEM((n_exp, capacity, width), bf16),
        pltpu.VMEM((n_exp, capacity, width), bf16),
        pltpu.VMEM(w_qkv.shape[1:], bf16),
        pltpu.VMEM(w_out.shape[1:], bf16),
        pltpu.VMEM((n_rep, width, hidden), bf16),
        pltpu.VMEM((n_rep, width, hidden), bf16),
        pltpu.VMEM((n_rep, hidden, width), bf16),
    ]
    semaphores = [(len(small),), (5,), (2 * n_head,), (2 * n_head,), (n_rep, 3), (n_rep, 3), (n_qp,), (n_qp,)]
    semaphores += [(2 * n_head,), (2 * n_head,), *[(n_exp,)] * 8]
    return pl.pallas_call(
        functools.partial(layer_kernel, (n_tok, n_qp, n_rep, main, tail, capacity, early, groups)),
        out_shape=pltpu.VMEM((block_rows, width), bf16),
        in_specs=[anywhere] * 11,
        out_specs=vmem,
        scratch_shapes=scratch + [pltpu.SemaphoreType.REGULAR] + [dma(shape) for shape in semaphores],
        compiler_params=pltpu.CompilerParams(
            collective_id=0, has_side_effects=True, vmem_limit_bytes=60 << 20
        ),
    )(
        *small,
        w_qkv,
        w_out,
        w_gate,
        w_up,
        w_down,
    )


def solution(mesh):
    in_specs = (
        P(("group", "tok", "qp", "rep"), None),
        P(("group", "tok", "qp", "rep"), None, None),
        P(("tok", "rep"), None, None),
        P(("tok", "rep"), None, None),
        P(("tok", "rep"), None),
        P(),
        P(("group", "tok", "qp", "rep"), None),
        P(("tok", "qp"), None),
        P(("tok", "qp"), None, "rep"),
        P(("tok", "qp"), None, "rep"),
        P(("tok", "qp"), "rep", None),
    )
    out_specs = P(("group", "tok", "qp", "rep"), None)
    sizes = (mesh.shape["tok"], mesh.shape["qp"], mesh.shape["rep"])
    return jax.shard_map(
        functools.partial(local, sizes), mesh=mesh, in_specs=in_specs, out_specs=out_specs, check_vma=False
    )
```
